128 devices in a mesh: blk: 64 (over z, y_lo, x, core), span: 2 (over y_hi).
Axes of the slice: x: 4, y: 4 (y_hi: 2, y_lo: 2; y = y_hi * 2 + y_lo), z: 4, core: 2. Of those that a mesh axis runs over, the one named last changes fastest.
Arguments:
- state_now: float32 [5, 9, 16, 1024, 128], P(None, None, 'span', 'blk'), may hold values from -6 to 6
- base_state: float32 [5, 9, 16, 1024, 128], P(None, None, 'span', 'blk'), may hold values from -6 to 6
- time_step: float32 [16, 1024, 128], P('span', 'blk'), may hold values from 0.05 to 0.3
- row_map: int32 [64], replicated, may hold values from 0 to 2, as said below
- lag_shift: int32 [3], replicated, may hold values from 1 to 8
- mode_count: int32 [2], replicated, may hold values from 8 to 16, as said below
- jacobian: float32 [3, 3, 5, 5], replicated, may hold values from -2.5 to 2.5
- dissipation: float32 [3, 3], replicated, may hold values from 0.2 to 1
- frequency: float32 [3], replicated, may hold values from 0.5 to 2
Outputs:
- state_next: float32 [5, 9, 16, 1024, 128], P(None, None, 'span', 'blk')
The draws below stay inside these ranges and needn't reach their ends.
Inputs may be any that keep to these rules, and one draw needn't show every extreme that they name: `row_map`: never falling; the 3 rows hold 2, 33 and the remaining blocks, in an order that varies. `mode_count`: one interface keeps exactly 16 modes.
All inputs are finite; a program needn't handle non-finite values.
Results may differ from the reference program's by a relative error of at most 0.00005.
Values sent between devices are 32-bit elements; how exact they have to be, the bound alone decides.
No kernel may reach another device: no remote copies, remote signals or barrier semaphores. Data moves between devices by JAX's collectives and lax.ppermute only.
A program may use at most 192 MiB of HBM per device.

```python
import math
import jax
import jax.numpy as jnp
from jax import lax

VARS = 5
INST = 9
ROWS = 3
MODES = 16
PCH = 16
AX = 128
NP = 1024
SPAN = 16
N_BLK = 64


def draw_row_map(key, part):
    widest = N_BLK // 2 + 1
    lengths = jnp.array([2, widest, N_BLK - widest - 2], dtype=jnp.int32)
    order = jax.random.permutation(jax.random.fold_in(key, 11), ROWS)
    counts = lengths[order]
    ends = jnp.cumsum(counts)
    block_ids = jnp.arange(N_BLK, dtype=jnp.int32)
    return jnp.sum((block_ids[:, None] >= ends[None, :]).astype(jnp.int32), axis=1).astype(jnp.int32)


def draw_mode_count(key, part):
    lower = jax.random.randint(jax.random.fold_in(key, 23), (ROWS - 1,), MODES // 2, MODES)
    chosen = jax.random.randint(jax.random.fold_in(key, 29), (), 0, ROWS - 1)
    return jnp.where(jnp.arange(ROWS - 1, dtype=jnp.int32) == chosen, MODES, lower).astype(jnp.int32)


def shard_levels(rng, shape, cuts, low, high):
    loudness, own = 1.0, jax.random.fold_in(rng, 6)
    for axis_at, parts in cuts:
        draws = jnp.exp(jax.random.uniform(jax.random.fold_in(own, axis_at), (parts,), jnp.float32, low / len(cuts), high / len(cuts)))
        loudness = loudness * jnp.repeat(draws, shape[axis_at] // parts).reshape([-1 if axis == axis_at else 1 for axis in range(len(shape))])
    return loudness


def scatter_about(stream_key, extent, deviation, reach, pieces=(), held_as=jnp.bfloat16):
    values = deviation * jax.random.normal(stream_key, extent, jnp.float32)
    if pieces:
        values = values * shard_levels(stream_key, extent, pieces, -0.22, 0.18)
    return jnp.clip(values, -reach, reach).astype(held_as)


def setup_inputs(seed: int = 0) -> dict:
    seeds = jax.random.split(jax.random.key(seed), 10)
    state_now = scatter_about(seeds[0], (VARS, INST, SPAN, NP, AX), 1.0, 6.0, ((2, 2), (3, 64)), jnp.float32)
    base_state = scatter_about(seeds[1], (VARS, INST, SPAN, NP, AX), 1.0, 6.0, ((2, 2), (3, 64)), jnp.float32)
    time_step = jnp.clip(jnp.exp(math.log(0.3) - 1.7917595 * jax.random.uniform(seeds[2], (SPAN, NP, AX), jnp.float32) ** shard_levels(seeds[2], (SPAN, NP, AX), ((0, 2), (1, 64)), -0.2, 0.2)), 0.05, 0.3)
    row_map = draw_row_map(jax.random.fold_in(seeds[9], 71), 0)
    lag_shift = jax.random.randint(seeds[4], (ROWS,), 1, INST).astype(jnp.int32)
    mode_count = draw_mode_count(jax.random.fold_in(seeds[9], 71), 0)
    jacobian = scatter_about(seeds[6], (ROWS, 3, VARS, VARS), VARS ** -0.5, 2.5, (), jnp.float32)
    dissipation = jnp.clip(jnp.exp(jax.random.uniform(seeds[7], (ROWS, 3), jnp.float32, math.log(0.2), math.log(1.0))), 0.2, 1.0)
    frequency = jnp.clip(jnp.exp(jax.random.uniform(seeds[8], (ROWS,), jnp.float32, math.log(0.5), math.log(2.0))), 0.5, 2.0)
    return {"state_now": state_now, "base_state": base_state, "time_step": time_step, "row_map": row_map, "lag_shift": lag_shift, "mode_count": mode_count, "jacobian": jacobian, "dissipation": dissipation, "frequency": frequency}


def spectral_table():
    row_ids = jnp.arange(INST, dtype=jnp.int32)[:, None]
    col_ids = jnp.arange(INST, dtype=jnp.int32)[None, :]
    offset = (row_ids - col_ids).astype(jnp.float32)
    on_diagonal = row_ids == col_ids
    denominator = jnp.where(on_diagonal, jnp.float32(1.0), jnp.sin(jnp.pi * offset / INST))
    return jnp.where(on_diagonal, jnp.float32(0.0), 0.5 * jnp.cos(jnp.pi * offset) / denominator)


def roll_table(shifts):
    source = (jnp.arange(INST, dtype=jnp.int32)[:, None] + shifts[None, :]) % INST
    return (source[:, None, :] == jnp.arange(INST, dtype=jnp.int32)[None, :, None]).astype(jnp.float32)


def reference(state_now, base_state, time_step, row_map, lag_shift, mode_count, jacobian, dissipation, frequency):
    exact = lax.Precision.HIGHEST
    columns = state_now.shape[3]
    axial = state_now.shape[4]
    col_ids = jnp.arange(columns, dtype=jnp.int32)
    row_ids = jnp.arange(ROWS, dtype=jnp.int32)
    column_row = row_map[col_ids // PCH]
    row_hot = (row_ids[:, None] == column_row[None, :]).astype(jnp.float32)
    block_total = jnp.sum((row_map[None, :] == row_ids[:, None]).astype(jnp.int32), axis=1)
    block_begin = jnp.cumsum(block_total) - block_total
    column_begin = block_begin[column_row] * PCH
    column_width = block_total[column_row] * PCH
    column_final = column_begin + column_width - 1
    left_index = jnp.where(col_ids > column_begin, col_ids - 1, column_final)
    right_index = jnp.where(col_ids < column_final, col_ids + 1, column_begin)
    column_lag = lag_shift[column_row]
    left_shift = jnp.where(col_ids == column_begin, column_lag, 0).astype(jnp.int32)
    right_shift = jnp.where(col_ids == column_final, -column_lag, 0).astype(jnp.int32)
    left_field = jnp.einsum('vksca,jkc->vjsca', jnp.take(state_now, left_index, axis=3), roll_table(left_shift), precision=exact)
    right_field = jnp.einsum('vksca,jkc->vjsca', jnp.take(state_now, right_index, axis=3), roll_table(right_shift), precision=exact)
    span_pad = jnp.pad(state_now, ((0, 0), (0, 0), (1, 1), (0, 0), (0, 0)))
    mode_ids = jnp.arange(MODES, dtype=jnp.int32)
    circle = column_width.astype(jnp.float32)
    angle = 2.0 * jnp.pi * ((col_ids - column_begin).astype(jnp.float32) + 0.5) / circle
    harmonic = mode_ids.astype(jnp.float32)[:, None] * angle[None, :]
    cos_basis = jnp.cos(harmonic)
    sin_basis = jnp.sin(harmonic)
    mode_weight = jnp.where(mode_ids == 0, 1.0, 2.0).astype(jnp.float32)[:, None] / circle[None, :]

    def project(face):
        cosine = jnp.einsum('vksc,mc,rc->rvksm', face, cos_basis * mode_weight, row_hot, precision=exact)
        sine = jnp.einsum('vksc,mc,rc->rvksm', face, sin_basis * mode_weight, row_hot, precision=exact)
        return cosine, sine

    outlet_cos, outlet_sin = project(state_now[..., axial - 1])
    inlet_cos, inlet_sin = project(state_now[..., 0])
    previous_hot = (row_ids[:, None] == column_row[None, :] - 1).astype(jnp.float32)
    next_hot = (row_ids[:, None] == column_row[None, :] + 1).astype(jnp.float32)
    inlet_limit = mode_count[jnp.clip(column_row - 1, 0, ROWS - 2)]
    outlet_limit = mode_count[jnp.clip(column_row, 0, ROWS - 2)]
    inlet_mask = (mode_ids[:, None] < inlet_limit[None, :]).astype(jnp.float32)
    outlet_mask = (mode_ids[:, None] < outlet_limit[None, :]).astype(jnp.float32)
    ghost_in = jnp.einsum('rvksm,rc,mc->vksc', outlet_cos, previous_hot, cos_basis * inlet_mask, precision=exact)
    ghost_in = ghost_in + jnp.einsum('rvksm,rc,mc->vksc', outlet_sin, previous_hot, sin_basis * inlet_mask, precision=exact)
    ghost_out = jnp.einsum('rvksm,rc,mc->vksc', inlet_cos, next_hot, cos_basis * outlet_mask, precision=exact)
    ghost_out = ghost_out + jnp.einsum('rvksm,rc,mc->vksc', inlet_sin, next_hot, sin_basis * outlet_mask, precision=exact)
    axial_pad = jnp.concatenate([ghost_in[..., None], state_now, ghost_out[..., None]], axis=4)
    column_jac = jacobian[column_row]
    column_dissip = dissipation[column_row]

    def direction_term(plus, minus, number):
        flux = 0.5 * jnp.einsum('cuv,vksca->uksca', column_jac[:, number], plus - minus, precision=exact)
        return flux - column_dissip[:, number][None, None, None, :, None] * (plus - 2.0 * state_now + minus)

    residual = direction_term(right_field, left_field, 0)
    residual = residual + direction_term(axial_pad[..., 2:], axial_pad[..., :-2], 1)
    residual = residual + direction_term(span_pad[:, :, 2:], span_pad[:, :, :-2], 2)
    spectral = frequency[column_row][None, None, None, :, None] * jnp.einsum('jk,vksca->vjsca', spectral_table(), state_now, precision=exact)
    return base_state - time_step[None, None] * (residual + spectral)
```

```python
import functools
import math

import jax
import jax.numpy as jnp
from jax import lax
from jax.experimental import pallas as pl
from jax.experimental.pallas import tpu as pltpu
from jax.sharding import Mesh
from jax.sharding import PartitionSpec as P

MODES = 16
BLK = ("blk_0", "blk_1", "blk_2", "blk_3")
ORDERS = ((2, 33, 29), (2, 29, 33), (33, 2, 29), (33, 29, 2), (29, 2, 33), (29, 33, 2))
EXACT = lax.Precision.HIGHEST
VMEM = pltpu.VMEM
F32 = jnp.float32
QUAD = (0, 1, 8, 9)
ACROSS_X = (2, 4, 6)
ACROSS_Z = (16, 32, 48)
DN = tuple(0.5 * math.cos(math.pi * n) / math.sin(math.pi * n / 9) for n in range(5) if n)


def vspec():
    return pl.BlockSpec(memory_space=VMEM)


def sspec():
    return pl.BlockSpec(memory_space=pltpu.SMEM)


def hspec():
    return pl.BlockSpec(memory_space=pl.ANY)


def own_block():
    return (
        (lax.axis_index("blk_0") * 2 + lax.axis_index("blk_1")) * 4 + lax.axis_index("blk_2")
    ) * 2 + lax.axis_index("blk_3")


def own_quarter():
    return lax.axis_index("blk_1") * 2 + lax.axis_index("blk_3")


def lengths_of(order):
    n0 = jnp.where(order < 2, 2, jnp.where(order < 4, 33, 29))
    n1 = jnp.where(
        (order == 2) | (order == 4), 2, jnp.where((order == 0) | (order == 5), 33, 29)
    )
    return n0, n1


def place_in_row(order, block):
    n0, n1 = lengths_of(order)
    row = (block >= n0).astype(jnp.int32) + (block >= n0 + n1).astype(jnp.int32)
    begin = jnp.where(row == 0, 0, jnp.where(row == 1, n0, n0 + n1))
    total = jnp.where(row == 0, n0, jnp.where(row == 1, n1, 64 - n0 - n1))
    return row, block - begin, total


def collect_kernel(rows_ref, x_hbm, order_ref, f0, f1, f2, f3, faces, rim_l, rim_r, edge, x, sem):
    copies = [
        pltpu.make_async_copy(x_hbm.at[pl.ds(9 * v, 9)], x.at[pl.ds(9 * v, 9)], sem.at[v])
        for v in range(5)
    ]
    for copy in copies:
        copy.start()
    late = rows_ref[31] == 2
    first = jnp.where(rows_ref[2] == 1, 0, jnp.where(rows_ref[29] == 0, 2, 4))
    second = jnp.where(
        first == 0,
        late.astype(jnp.int32),
        jnp.where(first == 2, (rows_ref[35] != 2).astype(jnp.int32), 1 - late.astype(jnp.int32)),
    )
    order_ref[0] = first + second
    lane = lax.broadcasted_iota(jnp.int32, (16, 128), 1) // 2
    upper = lax.axis_index("span")
    acc = [jnp.zeros((16, 128), F32) for _ in range(8)]
    for v in range(5):
        copies[v].wait()
        for k in range(9):
            j = v * 9 + k
            rim_l[j] = x[j, pl.ds(0, 8, stride=16), :]
            rim_r[j] = x[j, pl.ds(15, 8, stride=16), :]
            edge[j] = x[j, pl.ds(pl.multiple_of((1 - upper) * 112, 16), 16), :]
            for s in range(8):
                turned = pltpu.roll(x[j, pl.ds(16 * s, 16), :], 2 * j + 1, 1)
                acc[s] = jnp.where(lane == j, turned, acc[s])
    for s in range(8):
        faces[s] = acc[s]
    q = own_quarter()
    for d, ref in enumerate((f0, f1, f2, f3)):
        ref[...] = faces[pl.ds(2 * lax.bitwise_xor(q, d), 2)]


def basis_kernel(order_ref, jac_ref, dis_ref, forward, backward, mixing):
    order = order_ref[0]
    block = own_block()
    members = [place_in_row(order, lax.bitwise_xor(block, m)) for m in QUAD]

    def per_member(shape, dim):
        ids = lax.broadcasted_iota(jnp.int32, shape, dim)
        member = ids // 16
        pick = lambda n: functools.reduce(
            lambda a, d: jnp.where(member == d, members[d][n], a), range(1, 4), jnp.full(shape, members[0][n], jnp.int32)
        )
        row, position, total = pick(0), pick(1), pick(2)
        return row, (position * 16 + ids % 16) * 2 + 1, total * 32

    def harmonics(part_of, mode, odd, period):
        turns = lax.rem(mode * odd, period).astype(F32)
        angle = turns * (2.0 * math.pi) / period.astype(F32)
        return jnp.where(part_of == 0, jnp.cos(angle), jnp.sin(angle))

    shape = (32, 64)
    ids = lax.broadcasted_iota(jnp.int32, shape, 0)
    row, odd, period = per_member(shape, 1)
    mode = ids % 16
    wave = harmonics(ids // 16, mode, odd, period)
    wave = wave * jnp.where(mode == 0, 2.0, 4.0) / period.astype(F32)
    for r in range(3):
        forward[pl.ds(32 * r, 32), :] = jnp.where(row == r, wave, 0.0)
    shape = (64, 64)
    ids = lax.broadcasted_iota(jnp.int32, shape, 1)
    row, odd, period = per_member(shape, 0)
    wave = harmonics((ids // 16) % 2, ids % 16, odd, period)
    gap = ids // 32
    backward[pl.ds(0, 64), :] = jnp.where(gap == row - 1, wave, 0.0)
    backward[pl.ds(64, 64), :] = jnp.where(gap == row, wave, 0.0)
    own_row = members[0][0]
    shape = (128, 128)
    source = lax.broadcasted_iota(jnp.int32, shape, 0)
    target = lax.broadcasted_iota(jnp.int32, shape, 1)
    crossed = lax.bitwise_xor(target, 1)
    offset = crossed - source
    sign = jnp.where(source % 2 == 0, -0.5, 0.5)
    v_of = source // 18
    weight = jnp.zeros(shape, F32)
    for u in range(5):
        for v in range(5):
            here = (v_of == v) & (offset == 18 * (u - v)) & (source < 90)
            weight = jnp.where(here, jac_ref[own_row, 1, u, v], weight)
    weight = weight * sign - jnp.where((offset == 0) & (source < 90), dis_ref[own_row, 1], 0.0)
    mixing[...] = weight


def project_kernel(f0, f1, f2, f3, forward, out):
    even = lax.broadcasted_iota(jnp.int32, (32, 128), 1) % 2 == 0
    for i in range(2):
        columns = jnp.concatenate([f0[i], f1[i], f2[i], f3[i]], axis=0)
        parts = jnp.dot(forward[...], columns, precision=EXACT, preferred_element_type=F32)
        low, mid, high = parts[:32], parts[32:64], parts[64:]
        out[i, pl.ds(0, 32), :] = jnp.where(even, low, mid)
        out[i, pl.ds(32, 32), :] = jnp.where(even, mid, high)


def evaluate_kernel(count_ref, m0, m1, m2, m3, backward, g0, g1, g2, g3):
    ids = lax.broadcasted_iota(jnp.int32, (64, 128), 0)
    limit = jnp.where(ids < 32, count_ref[0], count_ref[1])
    kept = ids % 16 < limit
    even = lax.broadcasted_iota(jnp.int32, (64, 128), 1) % 2 == 0
    for i in range(2):
        modes = jnp.where(kept, (m0[i] + m1[i]) + (m2[i] + m3[i]), 0.0)
        both = jnp.dot(backward[...], modes, precision=EXACT, preferred_element_type=F32)
        ghost = jnp.where(even, both[:64], both[64:])
        for d, ref in enumerate((g0, g1, g2, g3)):
            ref[i] = ghost[16 * d : 16 * d + 16]


def stencil_kernel(
    order_ref, lag_ref, jac_ref, dis_ref, freq_ref, ghost_l, ghost_r, edge, x_hbm, base_hbm, dt,
    out, x, base, sem_x, sem_b,
):
    for s in range(8):
        pltpu.make_async_copy(
            x_hbm.at[:, pl.ds(16 * s, 16), :], x.at[:, pl.ds(24 * s + 32, 16), :], sem_x.at[s]
        ).start()
        pltpu.make_async_copy(
            base_hbm.at[:, pl.ds(16 * s, 16), :], base.at[:, pl.ds(16 * s, 16), :], sem_b.at[s]
        ).start()
    row, position, total = place_in_row(order_ref[0], own_block())
    lag = lag_ref[row]
    turn_l = jnp.where(position == 0, lag, 0)
    turn_r = jnp.where(position == total - 1, 9 - lag, 0)
    upper = lax.axis_index("span")
    keep_low = jnp.where(upper == 1, 1.0, 0.0)
    keep_high = jnp.where(upper == 0, 1.0, 0.0)

    @pl.loop(0, 9)
    def _(k):
        for v in range(5):
            j = v * 9 + k
            x[j, pl.ds(31, 8, stride=24), :] = ghost_l[v * 9 + lax.rem(k + turn_l, 9)]
            x[j, pl.ds(48, 8, stride=24), :] = ghost_r[v * 9 + lax.rem(k + turn_r, 9)]
            x[j, pl.ds(8, 16), :] = edge[j] * keep_low
            x[j, pl.ds(224, 16), :] = edge[j] * keep_high

    half = [
        [[0.5 * jac_ref[row, d, u, v] for v in range(5)] for u in range(5)] for d in range(3)
    ]
    eps = [dis_ref[row, d] for d in range(3)]
    centre = 2.0 * (eps[0] + eps[1] + eps[2])
    wave = [freq_ref[row] * DN[n] for n in range(4)]

    def wait(s):
        pltpu.make_async_copy(
            x_hbm.at[:, pl.ds(0, 16), :], x.at[:, pl.ds(24 * 0 + 32, 16), :], sem_x.at[s]
        ).wait()

    wait(0)

    @pl.loop(0, 8)
    def _(s):
        @pl.when(s < 7)
        def _():
            wait(s + 1)

        pltpu.make_async_copy(
            base_hbm.at[:, pl.ds(0, 16), :], base.at[:, pl.ds(0, 16), :], sem_b.at[s]
        ).wait()
        at = pl.multiple_of(24 * s + 32, 8)
        to = pl.multiple_of(16 * s, 16)
        for h in range(2):
            here, there = pl.ds(at + 8 * h, 8), pl.ds(to + 8 * h, 8)
            for u in range(5):
                line = [x[u * 9 + k, here, :] for k in range(9)]
                for k in range(9):
                    turn = [
                        (line[(k - n) % 9] - line[(k + n) % 9]) * wave[n - 1] for n in range(1, 5)
                    ]
                    out[u * 9 + k, there, :] = (turn[0] + turn[1]) + (turn[2] + turn[3])
            step = dt[there, :]
            for k in range(9):
                acc, diffs = [], []
                for v in range(5):
                    j = v * 9 + k
                    own = x[j, here, :]
                    left = x[j, pl.ds(at + 8 * h - 1, 8), :]
                    right = x[j, pl.ds(at + 8 * h + 1, 8), :]
                    before = pltpu.roll(own, 1, 1)
                    after = pltpu.roll(own, 127, 1)
                    below = x[j, pl.ds(at + 8 * h - 24, 8), :]
                    above = x[j, pl.ds(at + 8 * h + 24, 8), :]
                    diffs.append((right - left, after - before, above - below))
                    acc.append(
                        (out[j, there, :] + own * centre - (right + left) * eps[0])
                        - ((after + before) * eps[1] + (above + below) * eps[2])
                    )
                for u in range(5):
                    j = u * 9 + k
                    total_u = acc[u]
                    for d in range(3):
                        part = diffs[0][d] * half[d][u][0]
                        for v in range(1, 5):
                            part = part + diffs[v][d] * half[d][u][v]
                        total_u = total_u + part
                    out[j, there, :] = base[j, there, :] - step * total_u


def finish_kernel(acc, g0, g1, g2, g3, faces, mixing, dt, out_hbm, out, ghost, sem):
    q = own_quarter()
    for d, ref in enumerate((g0, g1, g2, g3)):
        for i in range(2):
            s = 2 * lax.bitwise_xor(q, d) + i
            ghost[pl.ds(pl.multiple_of(16 * s, 16), 16), :] = ref[i] - faces[s]
    terms = jnp.dot(ghost[...], mixing[...], precision=EXACT, preferred_element_type=F32)
    lane = lax.broadcasted_iota(jnp.int32, (128, 128), 1)
    terms = terms
    step = jnp.where((lane == 0) | (lane == 127), dt[...], 0.0)
    for v in range(5):
        @pl.loop(9 * v, 9 * v + 9)
        def _(j):
            turned = pltpu.roll(terms, 127 - 2 * j, 1)
            out[j] = acc[j] - step * turned

        pltpu.make_async_copy(
            out.at[pl.ds(9 * v, 9)], out_hbm.at[pl.ds(9 * v, 9)], sem.at[v]
        ).start()
    for v in range(5):
        pltpu.make_async_copy(
            out.at[pl.ds(9 * v, 9)], out_hbm.at[pl.ds(9 * v, 9)], sem.at[v]
        ).wait()


def swap(x, mask):
    return lax.ppermute(x, BLK, [(i, i ^ mask) for i in range(64)])


def ring(order):
    pairs, begin = [], 0
    for length in order:
        pairs += [(begin + i, begin + (i + 1) % length) for i in range(length)]
        begin += length
    return pairs


def sds(*shape, dtype=F32):
    return jax.ShapeDtypeStruct(shape, dtype)


def call(kernel, outs, in_specs, out_specs, scratch=(), limit=40, flops=0, name=None):
    return pl.pallas_call(
        kernel,
        out_shape=outs,
        in_specs=in_specs,
        out_specs=out_specs,
        scratch_shapes=list(scratch),
        name=name,
        cost_estimate=pl.CostEstimate(flops=flops, bytes_accessed=flops // 8, transcendentals=0),
        compiler_params=pltpu.CompilerParams(vmem_limit_bytes=limit << 20),
    )


def per_device(state, base, dt, row_map, lag, count, jac, dis, freq):
    shape = state.shape
    x = state.reshape(45, 128, 128)
    b = base.reshape(45, 128, 128)
    dt = dt.reshape(128, 128)
    quarter = sds(2, 16, 128)
    dma = pltpu.SemaphoreType.DMA
    order, f0, f1, f2, f3, faces, rim_l, rim_r, edge = call(
        collect_kernel,
        [sds(1, dtype=jnp.int32), quarter, quarter, quarter, quarter, sds(8, 16, 128)]
        + [sds(45, 8, 128), sds(45, 8, 128), sds(45, 16, 128)],
        [sspec(), hspec()],
        [sspec()] + [vspec()] * 8,
        [VMEM((45, 128, 128), F32), dma((5,))],
        name="collect",
    )(row_map, x)

    def branch(lengths):
        right = ring(lengths)
        left = [(t, s) for s, t in right]

        def run(order, f0, f1, f2, f3, faces, rim_l, rim_r, edge, x, b, dt, lag, count, jac, dis, freq):
            r = [swap(f, QUAD[d]) for d, f in ((1, f1), (2, f2), (3, f3))]
            from_left = lax.ppermute(rim_r, BLK, right)
            from_right = lax.ppermute(rim_l, BLK, left)
            from_span = lax.ppermute(edge, "span", [(0, 1), (1, 0)])
            forward, backward, mixing = call(
                basis_kernel,
                [sds(96, 64), sds(128, 64), sds(128, 128)],
                [sspec()] * 3,
                [vspec()] * 3,
                name="basis",
                flops=1000000,
            )(order, jac, dis)
            modes = call(
                project_kernel, sds(2, 64, 128), [vspec()] * 5, vspec(), name="project", flops=1000000
            )(f0, *r, forward)
            for masks in (ACROSS_X, ACROSS_Z):
                others = [swap(modes, m) for m in masks]
                if masks is ACROSS_X:
                    modes = (modes + others[0]) + (others[1] + others[2])
            acc = call(
                stencil_kernel,
                sds(45, 128, 128),
                [sspec()] * 5 + [vspec()] * 3 + [hspec()] * 2 + [vspec()],
                vspec(),
                [VMEM((45, 240, 128), F32), VMEM((45, 128, 128), F32), dma((8,)), dma((8,))],
                name="stencil",
                flops=50000000,
            )(order, lag, jac, dis, freq, from_left, from_right, from_span, x, b, dt)
            g = call(
                evaluate_kernel,
                [quarter] * 4,
                [sspec()] + [vspec()] * 5,
                [vspec()] * 4,
                name="evaluate",
                flops=1000000,
            )(count, modes, *others, backward)
            h = [swap(g[d], QUAD[d]) for d in (1, 2, 3)]
            return call(
                finish_kernel,
                sds(45, 128, 128),
                [vspec()] * 8,
                hspec(),
                [VMEM((45, 128, 128), F32), VMEM((128, 128), F32), dma((5,))],
                name="finish",
                flops=10000000,
            )(acc, g[0], *h, faces, mixing, dt)

        return run

    out = lax.switch(
        order[0],
        [branch(lengths) for lengths in ORDERS],
        order, f0, f1, f2, f3, faces, rim_l, rim_r, edge, x, b, dt, lag, count, jac, dis, freq,
    )
    return out.reshape(shape)


def solution(mesh):
    finer = Mesh(
        mesh.devices.reshape(4, 2, 4, 2, mesh.shape["span"]),
        ("blk_0", "blk_1", "blk_2", "blk_3", "span"),
    )
    return jax.shard_map(
        per_device,
        mesh=finer,
        in_specs=(
            P(None, None, "span", BLK, None),
            P(None, None, "span", BLK, None),
            P("span", BLK, None),
            P(),
            P(),
            P(),
            P(),
            P(),
            P(),
        ),
        out_specs=P(None, None, "span", BLK, None),
        check_vma=False,
    )
```

```python
import functools
import math

import jax
import jax.numpy as jnp
from jax import lax
from jax.experimental import pallas as pl
from jax.experimental.pallas import tpu as pltpu
from jax.sharding import Mesh
from jax.sharding import PartitionSpec as P

MODES = 16
BLK = ("blk_0", "blk_1", "blk_2", "blk_3")
ENDS = (
    ((0, 1), (35, 63), (2, 34), (33, 61), (29, 30)),
    ((0, 32), (31, 63), (2, 30), (33, 34), (29, 61)),
    ((0, 28), (62, 63)),
)
EXACT = lax.Precision.HIGHEST
VMEM = pltpu.VMEM
F32 = jnp.float32
QUAD = (0, 1, 8, 9)
ACROSS_X = (2, 4, 6)
ACROSS_Z = (16, 32, 48)
DN = tuple(0.5 * math.cos(math.pi * n) / math.sin(math.pi * n / 9) for n in range(5) if n)


CENTRE, WAVE, LEFT, RIGHT, SPAN, COEFS = 90, 91, 95, 96, 97, 99


def vspec():
    return pl.BlockSpec(memory_space=VMEM)


def sspec():
    return pl.BlockSpec(memory_space=pltpu.SMEM)


def hspec():
    return pl.BlockSpec(memory_space=pltpu.HBM)


def own_block():
    return (
        (lax.axis_index("blk_0") * 2 + lax.axis_index("blk_1")) * 4 + lax.axis_index("blk_2")
    ) * 2 + lax.axis_index("blk_3")


def own_quarter():
    return lax.axis_index("blk_1") * 2 + lax.axis_index("blk_3")


def lengths_of(order):
    n0 = jnp.where(order < 2, 2, jnp.where(order < 4, 33, 29))
    n1 = jnp.where(
        (order == 2) | (order == 4), 2, jnp.where((order == 0) | (order == 5), 33, 29)
    )
    return n0, n1


def place_in_row(order, block):
    n0, n1 = lengths_of(order)
    row = (block >= n0).astype(jnp.int32) + (block >= n0 + n1).astype(jnp.int32)
    begin = jnp.where(row == 0, 0, jnp.where(row == 1, n0, n0 + n1))
    total = jnp.where(row == 0, n0, jnp.where(row == 1, n1, 64 - n0 - n1))
    return row, block - begin, total


def sine_and_cosine(count, period):
    inverse = 1.0 / period
    rest = count - jnp.floor(count * inverse + 0.5) * period
    quarters = rest * (4.0 * inverse)
    turn = jnp.floor(quarters + 0.5)
    z = (quarters - turn) * (0.5 * math.pi)
    y = z * z
    sin = z * (1.0 + y * (-1 / 6 + y * (1 / 120 + y * (-1 / 5040 + y * (1 / 362880)))))
    cos = 1.0 + y * (
        -1 / 2 + y * (1 / 24 + y * (-1 / 720 + y * (1 / 40320 + y * (-1 / 3628800))))
    )
    turn = turn.astype(jnp.int32) & 3
    odd = (turn & 1) == 1
    sin, cos = jnp.where(odd, cos, sin), jnp.where(odd, sin, cos)
    return jnp.where(turn >= 2, -sin, sin), jnp.where((turn == 1) | (turn == 2), -cos, cos)


def write_tables(rows, lag, count, dis, freq, jac, forward, backward, mixing, coef):
    late = rows[31] == 2
    first = jnp.where(rows[2] == 1, 0, jnp.where(rows[29] == 0, 2, 4))
    second = jnp.where(
        first == 0,
        late.astype(jnp.int32),
        jnp.where(first == 2, (rows[35] != 2).astype(jnp.int32), 1 - late.astype(jnp.int32)),
    )
    order = first + second
    block = own_block()
    members = [place_in_row(order, lax.bitwise_xor(block, m)) for m in QUAD]
    row, position, total = members[0]

    shape = (16, 128)
    lane = lax.broadcasted_iota(jnp.int32, shape, 1)
    mode = lax.broadcasted_iota(jnp.int32, shape, 0)
    member = (lane // 16) & 3

    def pick(n):
        values = [jnp.full(shape, m[n], jnp.int32) for m in members]
        return jnp.where(
            member < 2,
            jnp.where(member == 0, values[0], values[1]),
            jnp.where(member == 2, values[2], values[3]),
        )

    its_row = pick(0)
    period = (pick(2) * 32).astype(F32)
    odd = ((pick(1) * 16 + (lane & 15)) * 2 + 1).astype(F32)
    sin, cos = sine_and_cosine(mode.astype(F32) * odd, period)
    weight = jnp.where(mode == 0, 2.0, 4.0) / period
    for r in range(3):
        here = its_row == r
        forward[pl.ds(32 * r, 16), :] = jnp.where(here, cos * weight, 0.0)[:, :64]
        forward[pl.ds(32 * r + 16, 16), :] = jnp.where(here, sin * weight, 0.0)[:, :64]
    seen = its_row - jnp.where(lane < 64, 1, 0)
    back = []
    for gap in range(2):
        kept = (seen == gap) & (mode < count[gap])
        back += [jnp.where(kept, cos, 0.0), jnp.where(kept, sin, 0.0)]
    backward[...] = jnp.concatenate(back, axis=0).T

    shape = (128, 128)
    source = lax.broadcasted_iota(jnp.int32, shape, 0)
    target = lax.broadcasted_iota(jnp.int32, shape, 1)

    def variable(ids):
        return sum((ids >= 18 * n).astype(jnp.int32) for n in range(1, 5))

    line = lax.broadcasted_iota(jnp.int32, (8, 128), 1)
    u_of = variable(line)
    v_of = variable(lax.broadcasted_iota(jnp.int32, (128, 1), 0))
    crossed = lax.bitwise_xor(target, 1)
    same = (crossed - 18 * u_of[:1]) == (source - 18 * v_of)
    terms = jnp.zeros(shape, F32)
    for v in range(5):
        entries = jnp.zeros((8, 128), F32)
        for u in range(5):
            entries = jnp.where(u_of == u, jac[row, u, 1, v], entries)
        terms = jnp.where(v_of == v, entries[:1], terms)
    terms = terms * jnp.where((source & 1) == 0, -0.5, 0.5)
    terms = terms - jnp.where(crossed == source, dis[row, 1], 0.0)
    mixing[...] = jnp.where(same & (source < 90), terms, 0.0)

    def put(at, value):
        coef[at] = jnp.full((8, 128), value, F32)

    for d in range(3):
        for u in range(5):
            for v in range(5):
                half = 0.5 * jac[row, u, d, v]
                if u == v:
                    put(75 + d * 5 + u, half - dis[row, d])
                    put(d * 25 + u * 5 + v, half + dis[row, d])
                else:
                    put(d * 25 + u * 5 + v, half)
    put(CENTRE, 2.0 * (dis[row, 0] + dis[row, 1] + dis[row, 2]))
    for n in range(4):
        put(WAVE + n, freq[row] * DN[n])
    begin = block - position
    which = jnp.where(
        total == 2,
        jnp.where(begin == 33, 1, jnp.where(begin == 62, 2, 0)),
        jnp.where(
            total == 33,
            jnp.where(begin == 2, 0, 1),
            jnp.where(begin == 0, 2, jnp.where(begin == 2, 1, 0)),
        ),
    )
    at_begin, at_final = position == 0, position == total - 1
    put(LEFT, jnp.where(at_begin, which, 3).astype(F32))
    put(RIGHT, jnp.where(at_final, which, 3).astype(F32))
    upper = lax.axis_index("span")
    put(SPAN, upper.astype(F32))
    put(SPAN + 1, (1 - upper).astype(F32))
    return at_begin, lag[row]


def collect_kernel(
    rows_hbm, lag_hbm, count_hbm, dis_hbm, freq_hbm, jac_hbm, x_hbm,
    f0, f1, f2, f3, faces, rim_l, rim_r, rim_w, edge, x, forward, backward, mixing, coef,
    rows, lag, count, dis, freq, jac, sem_p, sem,
):
    small = [
        pltpu.make_async_copy(a, b, sem_p.at[n])
        for n, (a, b) in enumerate(
            (
                (rows_hbm, rows), (lag_hbm, lag), (count_hbm, count),
                (dis_hbm, dis), (freq_hbm, freq), (jac_hbm, jac),
            )
        )
    ]
    copies = [
        pltpu.make_async_copy(
            x_hbm.at[:, pl.ds(16 * s, 16), :], x.at[:, pl.ds(24 * s + 32, 16), :], sem.at[s]
        )
        for s in range(8)
    ]
    for copy in small + copies:
        copy.start()
    for copy in small:
        copy.wait()
    at_begin, shift = write_tables(
        rows, lag, count, dis, freq, jac, forward, backward, mixing, coef
    )
    lane = lax.broadcasted_iota(jnp.int32, (8, 128), 1) // 2
    for s in range(8):
        copies[s].wait()
        acc = [jnp.zeros((8, 128), F32) for _ in range(2)]
        for j in range(45):
            for h in range(2):
                turned = pltpu.roll(x[j, pl.ds(24 * s + 32 + 8 * h, 8), :], 2 * j + 1, 1)
                acc[h] = jnp.where(lane == j, turned, acc[h])
        for h in range(2):
            faces[s, pl.ds(8 * h, 8), :] = acc[h]
    q = own_quarter()
    for d, ref in enumerate((f0, f1, f2, f3)):
        ref[...] = faces[pl.ds(2 * lax.bitwise_xor(q, d), 2)]
    turn = jnp.where(at_begin, 9 - shift, shift)
    end = jnp.where(at_begin, 32, 47)
    outer = pl.multiple_of(jnp.where(lax.axis_index("span") == 0, 200, 32), 8)

    @pl.loop(0, 9)
    def _(k):
        for v in range(5):
            j = v * 9 + k
            rim_l[j] = x[j, pl.ds(32, 8, stride=24), :]
            rim_r[j] = x[j, pl.ds(47, 8, stride=24), :]
            rim_w[j] = x[v * 9 + lax.rem(k + turn, 9), pl.ds(end, 8, stride=24), :]
            edge[j] = x[j, pl.ds(outer, 16), :]


def project_kernel(f0, f1, f2, f3, forward, out):
    even = lax.broadcasted_iota(jnp.int32, (32, 128), 1) % 2 == 0
    for i in range(2):
        columns = jnp.concatenate([f0[i], f1[i], f2[i], f3[i]], axis=0)
        parts = jnp.dot(forward[...], columns, precision=EXACT, preferred_element_type=F32)
        low, mid, high = parts[:32], parts[32:64], parts[64:]
        out[i, pl.ds(0, 32), :] = jnp.where(even, low, mid)
        out[i, pl.ds(32, 32), :] = jnp.where(even, mid, high)


def evaluate_kernel(m0, m1, m2, m3, backward, g0, g1, g2, g3):
    even = lax.broadcasted_iota(jnp.int32, (64, 128), 1) % 2 == 0
    for i in range(2):
        modes = (m0[i] + m1[i]) + (m2[i] + m3[i])
        both = jnp.dot(backward[...], modes, precision=EXACT, preferred_element_type=F32)
        ghost = jnp.where(even, both[:64], both[64:])
        for d, ref in enumerate((g0, g1, g2, g3)):
            ref[i] = ghost[16 * d : 16 * d + 16]


def stencil_kernel(
    coef, ghost_l, ghost_r, wrap0, wrap1, wrap2, edge, x_in, dt, base_hbm,
    out, x, base, sem_b,
):
    def fetch(s):
        rows = pl.ds(pl.multiple_of(16 * s, 16), 16)
        return pltpu.make_async_copy(base_hbm.at[:, rows, :], base.at[:, rows, :], sem_b.at[s])

    for s in range(8):
        fetch(s).start()
    left, right = coef[LEFT], coef[RIGHT]
    keep_low = jnp.concatenate([coef[SPAN]] * 2, axis=0)
    keep_high = jnp.concatenate([coef[SPAN + 1]] * 2, axis=0)

    @pl.loop(0, 9)
    def _(k):
        for v in range(5):
            j = v * 9 + k
            low, high = ghost_l[j], ghost_r[j]
            for w, wrap in enumerate((wrap0, wrap1, wrap2)):
                low = jnp.where(left == w, wrap[j], low)
                high = jnp.where(right == w, wrap[j], high)
            x[j, pl.ds(31, 8, stride=24), :] = low
            x[j, pl.ds(48, 8, stride=24), :] = high
            x[j, pl.ds(8, 16), :] = edge[j] * keep_low
            x[j, pl.ds(224, 16), :] = edge[j] * keep_high

    @pl.loop(0, 8)
    def _(s):
        fetch(s).wait()
        at = pl.multiple_of(24 * s + 32, 8)
        to = pl.multiple_of(16 * s, 16)
        for h in range(2):
            here, there = pl.ds(at + 8 * h, 8), pl.ds(to + 8 * h, 8)
            for u in range(5):
                line = [x[u * 9 + k, here, :] for k in range(9)]
                for k in range(9):
                    turn = [
                        (line[(k - n) % 9] - line[(k + n) % 9]) * coef[WAVE + n - 1]
                        for n in range(1, 5)
                    ]
                    out[u * 9 + k, there, :] = (turn[0] + turn[1]) + (turn[2] + turn[3])
            step = dt[there, :]
            for k in range(9):
                acc, diffs = [], []
                for v in range(5):
                    j = v * 9 + k
                    own = x[j, here, :]
                    pairs = (
                        (x[j, pl.ds(at + 8 * h + 1, 8), :], x[j, pl.ds(at + 8 * h - 1, 8), :]),
                        (pltpu.roll(own, 127, 1), pltpu.roll(own, 1, 1)),
                        (x[j, pl.ds(at + 8 * h + 24, 8), :], x[j, pl.ds(at + 8 * h - 24, 8), :]),
                    )
                    diffs.append([plus - minus for plus, minus in pairs])
                    term = out[j, there, :] + own * coef[CENTRE]
                    for d, (plus, minus) in enumerate(pairs):
                        term = term + (
                            plus * coef[75 + d * 5 + v] - minus * coef[d * 25 + v * 6]
                        )
                    acc.append(term)
                for u in range(5):
                    j = u * 9 + k
                    total_u = acc[u]
                    for d in range(3):
                        part = None
                        for v in range(5):
                            if v != u:
                                product = diffs[v][d] * coef[d * 25 + u * 5 + v]
                                part = product if part is None else part + product
                        total_u = total_u + part
                    out[j, there, :] = base[j, there, :] - step * total_u


def finish_kernel(acc, g0, g1, g2, g3, faces, mixing, dt, out_hbm, out, ghost, sem):
    q = own_quarter()
    for d, ref in enumerate((g0, g1, g2, g3)):
        for i in range(2):
            s = 2 * lax.bitwise_xor(q, d) + i
            ghost[pl.ds(pl.multiple_of(16 * s, 16), 16), :] = ref[i] - faces[s]
    terms = jnp.dot(ghost[...], mixing[...], precision=EXACT, preferred_element_type=F32)
    lane = lax.broadcasted_iota(jnp.int32, (128, 128), 1)
    step = jnp.where((lane == 0) | (lane == 127), dt[...], 0.0)
    for v in range(5):
        @pl.loop(9 * v, 9 * v + 9, step=3)
        def _(first):
            for j in (first, first + 1, first + 2):
                turned = pltpu.roll(terms, 127 - 2 * j, 1)
                out[j] = acc[j] - step * turned

        pltpu.make_async_copy(
            out.at[pl.ds(9 * v, 9)], out_hbm.at[pl.ds(9 * v, 9)], sem.at[v]
        ).start()
    for v in range(5):
        pltpu.make_async_copy(
            out.at[pl.ds(9 * v, 9)], out_hbm.at[pl.ds(9 * v, 9)], sem.at[v]
        ).wait()


def swap(x, mask):
    return lax.ppermute(x, BLK, [(i, i ^ mask) for i in range(64)])


def sds(*shape, dtype=F32):
    return jax.ShapeDtypeStruct(shape, dtype)


def call(kernel, outs, in_specs, out_specs, scratch=(), limit=24, flops=0, name=None, aliases={}):
    return pl.pallas_call(
        kernel,
        out_shape=outs,
        in_specs=in_specs,
        out_specs=out_specs,
        scratch_shapes=list(scratch),
        name=name,
        input_output_aliases=aliases,
        cost_estimate=pl.CostEstimate(flops=flops, bytes_accessed=flops // 8, transcendentals=0),
        compiler_params=pltpu.CompilerParams(vmem_limit_bytes=limit << 20),
    )


def per_device(state, base, dt, row_map, lag, count, jac, dis, freq):
    shape = state.shape
    x = state.reshape(45, 128, 128)
    b = base.reshape(45, 128, 128)
    dt = dt.reshape(128, 128)
    jac = jac.transpose(0, 2, 1, 3)
    x, b, row_map, lag, count, dis, freq, jac = [
        pltpu.with_memory_space_constraint(a, pltpu.HBM)
        for a in (x, b, row_map, lag, count, dis, freq, jac)
    ]
    quarter, rim = sds(2, 16, 128), sds(45, 8, 128)
    dma = pltpu.SemaphoreType.DMA
    padded = sds(45, 240, 128)
    f0, f1, f2, f3, faces, rim_l, rim_r, rim_w, edge, x, forward, backward, mixing, coef = call(
        collect_kernel,
        [quarter, quarter, quarter, quarter, sds(8, 16, 128), rim, rim, rim, sds(45, 16, 128)]
        + [padded, sds(96, 64), sds(128, 64), sds(128, 128), sds(COEFS, 8, 128)],
        [hspec()] * 7,
        [vspec()] * 14,
        [
            pltpu.SMEM((64,), jnp.int32),
            pltpu.SMEM((3,), jnp.int32),
            pltpu.SMEM((2,), jnp.int32),
            pltpu.SMEM((3, 3), F32),
            pltpu.SMEM((3,), F32),
            pltpu.SMEM((3, 5, 3, 5), F32),
            dma((6,)),
            dma((8,)),
        ],
        name="collect",
    )(row_map, lag, count, dis, freq, jac, x)
    r = [swap(f, QUAD[d]) for d, f in ((1, f1), (2, f2), (3, f3))]
    from_left = lax.ppermute(rim_r, BLK, [(i, (i + 1) % 64) for i in range(64)])
    from_right = lax.ppermute(rim_l, BLK, [((i + 1) % 64, i) for i in range(64)])
    wraps = [lax.ppermute(rim_w, BLK, [*pairs, *((b, a) for a, b in pairs)]) for pairs in ENDS]
    from_span = lax.ppermute(edge, "span", [(0, 1), (1, 0)])
    modes = call(
        project_kernel, sds(2, 64, 128), [vspec()] * 5, vspec(), name="project", flops=1000000
    )(f0, *r, forward)
    for masks in (ACROSS_X, ACROSS_Z):
        others = [swap(modes, m) for m in masks]
        if masks is ACROSS_X:
            modes = (modes + others[0]) + (others[1] + others[2])
    acc, _ = call(
        stencil_kernel,
        [sds(45, 128, 128), padded],
        [vspec()] * 9 + [hspec()],
        [vspec()] * 2,
        [VMEM((45, 128, 128), F32), dma((8,))],
        name="stencil",
        flops=50000000,
        aliases={7: 1},
    )(coef, from_left, from_right, *wraps, from_span, x, dt, b)
    g = call(
        evaluate_kernel,
        [quarter] * 4,
        [vspec()] * 5,
        [vspec()] * 4,
        name="evaluate",
        flops=1000000,
    )(modes, *others, backward)
    h = [swap(g[d], QUAD[d]) for d in (1, 2, 3)]
    out = call(
        finish_kernel,
        sds(45, 128, 128),
        [vspec()] * 8,
        hspec(),
        [VMEM((45, 128, 128), F32), VMEM((128, 128), F32), dma((5,))],
        name="finish",
        flops=10000000,
    )(acc, g[0], *h, faces, mixing, dt)
    return out.reshape(shape)


def solution(mesh):
    finer = Mesh(
        mesh.devices.reshape(4, 2, 4, 2, mesh.shape["span"]),
        ("blk_0", "blk_1", "blk_2", "blk_3", "span"),
    )
    return jax.shard_map(
        per_device,
        mesh=finer,
        in_specs=(
            P(None, None, "span", BLK, None),
            P(None, None, "span", BLK, None),
            P("span", BLK, None),
            P(),
            P(),
            P(),
            P(),
            P(),
            P(),
        ),
        out_specs=P(None, None, "span", BLK, None),
        check_vma=False,
    )
```

```python
import functools
import math

import jax
import jax.numpy as jnp
from jax import lax
from jax.experimental import pallas as pl
from jax.experimental.pallas import tpu as pltpu
from jax.sharding import Mesh
from jax.sharding import PartitionSpec as P

BLK = ("blk_0", "blk_1", "blk_2", "blk_3")
ORDERS = ((2, 33, 29), (2, 29, 33), (33, 2, 29), (33, 29, 2), (29, 2, 33), (29, 33, 2))
EXACT = lax.Precision.HIGHEST
VMEM = pltpu.VMEM
F32 = jnp.float32
QUAD = (0, 1, 8, 9)
HOPS = (2, 6, 16, 48)
DN = tuple(0.5 * math.cos(math.pi * n) / math.sin(math.pi * n / 9) for n in range(5) if n)


ALONG = ((0, 5), (5, 8))
ACROSS = ((0, 2), (2, 8))
CENTRE, WAVE, SPAN, COEFS = 90, 91, 95, 97


def vspec():
    return pl.BlockSpec(memory_space=VMEM)


def sspec():
    return pl.BlockSpec(memory_space=pltpu.SMEM)


def hspec():
    return pl.BlockSpec(memory_space=pltpu.HBM)


def own_block():
    return (
        (lax.axis_index("blk_0") * 2 + lax.axis_index("blk_1")) * 4 + lax.axis_index("blk_2")
    ) * 2 + lax.axis_index("blk_3")


def own_quarter():
    return lax.axis_index("blk_1") * 2 + lax.axis_index("blk_3")


def lengths_of(order):
    n0 = jnp.where(order < 2, 2, jnp.where(order < 4, 33, 29))
    n1 = jnp.where(
        (order == 2) | (order == 4), 2, jnp.where((order == 0) | (order == 5), 33, 29)
    )
    return n0, n1


def place_in_row(order, block):
    n0, n1 = lengths_of(order)
    row = (block >= n0).astype(jnp.int32) + (block >= n0 + n1).astype(jnp.int32)
    begin = jnp.where(row == 0, 0, jnp.where(row == 1, n0, n0 + n1))
    total = jnp.where(row == 0, n0, jnp.where(row == 1, n1, 64 - n0 - n1))
    return row, block - begin, total


def sine_and_cosine(count, period):
    inverse = 1.0 / period
    rest = count - jnp.floor(count * inverse + 0.5) * period
    quarters = rest * (4.0 * inverse)
    turn = jnp.floor(quarters + 0.5)
    z = (quarters - turn) * (0.5 * math.pi)
    y = z * z
    sin = z * (1.0 + y * (-1 / 6 + y * (1 / 120 + y * (-1 / 5040 + y * (1 / 362880)))))
    cos = 1.0 + y * (
        -1 / 2 + y * (1 / 24 + y * (-1 / 720 + y * (1 / 40320 + y * (-1 / 3628800))))
    )
    turn = turn.astype(jnp.int32) & 3
    odd = (turn & 1) == 1
    sin, cos = jnp.where(odd, cos, sin), jnp.where(odd, sin, cos)
    return jnp.where(turn >= 2, -sin, sin), jnp.where((turn == 1) | (turn == 2), -cos, cos)


def order_of(rows):
    late = rows[31] == 2
    first = jnp.where(rows[2] == 1, 0, jnp.where(rows[29] == 0, 2, 4))
    second = jnp.where(
        first == 0,
        late.astype(jnp.int32),
        jnp.where(first == 2, (rows[35] != 2).astype(jnp.int32), 1 - late.astype(jnp.int32)),
    )
    return first + second


def waves(members):
    shape = (16, 128)
    lane = lax.broadcasted_iota(jnp.int32, shape, 1)
    mode = lax.broadcasted_iota(jnp.int32, shape, 0)
    member = (lane // 16) & 3

    def pick(n):
        values = [jnp.full(shape, m[n], jnp.int32) for m in members]
        return jnp.where(
            member < 2,
            jnp.where(member == 0, values[0], values[1]),
            jnp.where(member == 2, values[2], values[3]),
        )

    its_row = pick(0)
    period = (pick(2) * 32).astype(F32)
    odd = ((pick(1) * 16 + (lane & 15)) * 2 + 1).astype(F32)
    sin, cos = sine_and_cosine(mode.astype(F32) * odd, period)
    return its_row, lane, mode, period, cos, sin


def members_of(order):
    block = own_block()
    return [place_in_row(order, lax.bitwise_xor(block, m)) for m in QUAD]


def write_forward(members, forward):
    its_row, _, mode, period, cos, sin = waves(members)
    weight = jnp.where(mode == 0, 2.0, 4.0) / period
    for r in range(3):
        here = its_row == r
        forward[pl.ds(32 * r, 16), :] = jnp.where(here, cos * weight, 0.0)[:, :64]
        forward[pl.ds(32 * r + 16, 16), :] = jnp.where(here, sin * weight, 0.0)[:, :64]


def write_rest(members, count, dis, freq, jac, backward, mixing, coef):
    row = members[0][0]
    its_row, lane, mode, _, cos, sin = waves(members)
    seen = its_row - jnp.where(lane < 64, 1, 0)
    back = []
    for gap in range(2):
        kept = (seen == gap) & (mode < count[gap])
        back += [jnp.where(kept, cos, 0.0), jnp.where(kept, sin, 0.0)]
    backward[...] = jnp.concatenate(back, axis=0).T

    shape = (128, 128)
    source = lax.broadcasted_iota(jnp.int32, shape, 0)
    target = lax.broadcasted_iota(jnp.int32, shape, 1)

    def variable(ids):
        return sum((ids >= 18 * n).astype(jnp.int32) for n in range(1, 5))

    line = lax.broadcasted_iota(jnp.int32, (8, 128), 1)
    u_of = variable(line)
    v_of = variable(lax.broadcasted_iota(jnp.int32, (128, 1), 0))
    crossed = lax.bitwise_xor(target, 1)
    same = (crossed - 18 * u_of[:1]) == (source - 18 * v_of)
    terms = jnp.zeros(shape, F32)
    for v in range(5):
        entries = jnp.zeros((8, 128), F32)
        for u in range(5):
            entries = jnp.where(u_of == u, jac[row, u, 1, v], entries)
        terms = jnp.where(v_of == v, entries[:1], terms)
    terms = terms * jnp.where((source & 1) == 0, -0.5, 0.5)
    terms = terms - jnp.where(crossed == source, dis[row, 1], 0.0)
    mixing[...] = jnp.where(same & (source < 90), terms, 0.0)

    def put(at, value):
        coef[at] = jnp.full((8, 128), value, F32)

    for d in range(3):
        for u in range(5):
            for v in range(5):
                half = 0.5 * jac[row, u, d, v]
                if u == v:
                    put(75 + d * 5 + u, half - dis[row, d])
                    put(d * 25 + u * 5 + v, half + dis[row, d])
                else:
                    put(d * 25 + u * 5 + v, half)
    put(CENTRE, 2.0 * (dis[row, 0] + dis[row, 1] + dis[row, 2]))
    for n in range(4):
        put(WAVE + n, freq[row] * DN[n])
    upper = lax.axis_index("span")
    put(SPAN, upper.astype(F32))
    put(SPAN + 1, (1 - upper).astype(F32))


def faces_kernel(x_hbm, f0, f1, f2, f3, faces, x, sem):
    copies = [
        pltpu.make_async_copy(
            x_hbm.at[:, pl.ds(16 * s, 16), :], x.at[:, pl.ds(24 * s + 32, 16), :], sem.at[s]
        )
        for s in range(8)
    ]
    for copy in copies:
        copy.start()
    lane = lax.broadcasted_iota(jnp.int32, (8, 128), 1) // 2
    for s in range(8):
        copies[s].wait()
        acc = [jnp.zeros((8, 128), F32) for _ in range(2)]
        for j in range(45):
            for h in range(2):
                turned = pltpu.roll(x[j, pl.ds(24 * s + 32 + 8 * h, 8), :], 2 * j + 1, 1)
                acc[h] = jnp.where(lane == j, turned, acc[h])
        for h in range(2):
            faces[s, pl.ds(8 * h, 8), :] = acc[h]
    q = own_quarter()
    for d, ref in enumerate((f0, f1, f2, f3)):
        ref[...] = faces[pl.ds(2 * lax.bitwise_xor(q, d), 2)]


def leave_kernel(
    rows_hbm, lag_hbm, x, order_ref, rim_l, rim_r, edge, forward, rows, lag, sem
):
    small = [
        pltpu.make_async_copy(a, b, sem.at[n])
        for n, (a, b) in enumerate(((rows_hbm, rows), (lag_hbm, lag)))
    ]
    for copy in small:
        copy.start()
    outer = pl.multiple_of(jnp.where(lax.axis_index("span") == 0, 200, 32), 8)

    @pl.loop(0, 9)
    def _(k):
        for v in range(5):
            edge[v * 9 + k] = x[v * 9 + k, pl.ds(outer, 16), :]

    for copy in small:
        copy.wait()
    order = order_of(rows)
    order_ref[0] = order
    members = members_of(order)
    write_forward(members, forward)
    row, position, total = members[0]
    turn_left = jnp.where(position == 0, 9 - lag[row], 0)
    turn_right = jnp.where(position == total - 1, lag[row], 0)

    @pl.loop(0, 9)
    def _(k):
        for v in range(5):
            j = v * 9 + k
            rim_l[j] = x[v * 9 + lax.rem(k + turn_left, 9), pl.ds(32, 8, stride=24), :]
            rim_r[j] = x[v * 9 + lax.rem(k + turn_right, 9), pl.ds(47, 8, stride=24), :]


def tables_kernel(
    rows_hbm, count_hbm, dis_hbm, freq_hbm, jac_hbm, x_hbm,
    x, backward, mixing, coef, rows, count, dis, freq, jac, sem, sem_x,
):
    small = [
        pltpu.make_async_copy(a, b, sem.at[n])
        for n, (a, b) in enumerate(
            (
                (rows_hbm, rows), (count_hbm, count),
                (dis_hbm, dis), (freq_hbm, freq), (jac_hbm, jac),
            )
        )
    ]
    copies = [
        pltpu.make_async_copy(
            x_hbm.at[:, pl.ds(16 * s, 16), :], x.at[:, pl.ds(24 * s + 32, 16), :], sem_x.at[s]
        )
        for s in range(8)
    ]
    for copy in small + copies:
        copy.start()
    for copy in small:
        copy.wait()
    write_rest(members_of(order_of(rows)), count, dis, freq, jac, backward, mixing, coef)
    for copy in copies:
        copy.wait()


def project_kernel(f0, f1, f2, f3, forward, out):
    even = lax.broadcasted_iota(jnp.int32, (32, 128), 1) % 2 == 0
    for i in range(2):
        columns = jnp.concatenate([f0[i], f1[i], f2[i], f3[i]], axis=0)
        parts = jnp.dot(forward[...], columns, precision=EXACT, preferred_element_type=F32)
        low, mid, high = parts[:32], parts[32:64], parts[64:]
        out[i, pl.ds(0, 32), :] = jnp.where(even, low, mid)
        out[i, pl.ds(32, 32), :] = jnp.where(even, mid, high)


def evaluate_kernel(m0, m1, backward, g0, g1, g2, g3):
    even = lax.broadcasted_iota(jnp.int32, (64, 128), 1) % 2 == 0
    for i in range(2):
        modes = m0[i] + m1[i]
        both = jnp.dot(backward[...], modes, precision=EXACT, preferred_element_type=F32)
        ghost = jnp.where(even, both[:64], both[64:])
        for d, ref in enumerate((g0, g1, g2, g3)):
            ref[i] = ghost[16 * d : 16 * d + 16]


def ghosts_kernel(coef, ghost_l, ghost_r, edge, x_in, x):
    keep_low = jnp.concatenate([coef[SPAN]] * 2, axis=0)
    keep_high = jnp.concatenate([coef[SPAN + 1]] * 2, axis=0)

    @pl.loop(0, 9)
    def _(k):
        for v in range(5):
            j = v * 9 + k
            x[j, pl.ds(31, 8, stride=24), :] = ghost_l[j]
            x[j, pl.ds(48, 8, stride=24), :] = ghost_r[j]
            x[j, pl.ds(8, 16), :] = edge[j] * keep_low
            x[j, pl.ds(224, 16), :] = edge[j] * keep_high


def across_kernel(first, last, coef, x, dt, base, out_in, out):
    @pl.loop(first, last)
    def _(s):
        at = pl.multiple_of(24 * s + 32, 8)
        to = pl.multiple_of(16 * s, 16)
        for h in range(2):
            there = pl.ds(to + 8 * h, 8)
            step = dt[there, :]
            for k in range(9):
                acc, diffs = [], []
                for v in range(5):
                    j = v * 9 + k
                    pairs = [
                        (d, x[j, pl.ds(at + 8 * h + r, 8), :], x[j, pl.ds(at + 8 * h - r, 8), :])
                        for d, r in ((0, 1), (2, 24))
                    ]
                    diffs.append({d: plus - minus for d, plus, minus in pairs})
                    terms = [
                        plus * coef[75 + d * 5 + v] - minus * coef[d * 25 + v * 6]
                        for d, plus, minus in pairs
                    ]
                    acc.append(terms[0] + terms[1])
                for u in range(5):
                    j = u * 9 + k
                    total_u = out[j, there, :] + acc[u]
                    for d in (0, 2):
                        part = None
                        for v in range(5):
                            if v != u:
                                product = diffs[v][d] * coef[d * 25 + u * 5 + v]
                                part = product if part is None else part + product
                        total_u = total_u + part
                    out[j, there, :] = base[j, there, :] - step * total_u


def along_first_kernel(first, last, coef, x, base_hbm, out, base, sem):
    fetch = pltpu.make_async_copy(base_hbm, base, sem)
    fetch.start()
    along_kernel(first, last, coef, x, out)
    fetch.wait()


def along_kernel(first, last, coef, x, *refs):
    out = refs[-1]

    @pl.loop(first, last)
    def _(s):
        at = pl.multiple_of(24 * s + 32, 8)
        to = pl.multiple_of(16 * s, 16)
        for h in range(2):
            here, there = pl.ds(at + 8 * h, 8), pl.ds(to + 8 * h, 8)
            for u in range(5):
                line = [x[u * 9 + k, here, :] for k in range(9)]
                for k in range(9):
                    turn = [
                        (line[(k - n) % 9] - line[(k + n) % 9]) * coef[WAVE + n - 1]
                        for n in range(1, 5)
                    ]
                    turn.append(line[k] * coef[CENTRE])
                    out[u * 9 + k, there, :] = (turn[0] + turn[1]) + (turn[2] + turn[3]) + turn[4]
            for k in range(9):
                acc, diffs = [], []
                for v in range(5):
                    j = v * 9 + k
                    own = x[j, here, :]
                    plus, minus = pltpu.roll(own, 127, 1), pltpu.roll(own, 1, 1)
                    diffs.append(plus - minus)
                    acc.append(
                        out[j, there, :]
                        + (plus * coef[80 + v] - minus * coef[25 + v * 6])
                    )
                for u in range(5):
                    part = None
                    for v in range(5):
                        if v != u:
                            product = diffs[v] * coef[25 + u * 5 + v]
                            part = product if part is None else part + product
                    out[u * 9 + k, there, :] = acc[u] + part


def finish_kernel(acc, g0, g1, g2, g3, faces, mixing, dt, out_hbm, out, ghost, sem):
    q = own_quarter()
    for d, ref in enumerate((g0, g1, g2, g3)):
        for i in range(2):
            s = 2 * lax.bitwise_xor(q, d) + i
            ghost[pl.ds(pl.multiple_of(16 * s, 16), 16), :] = ref[i] - faces[s]
    terms = jnp.dot(ghost[...], mixing[...], precision=EXACT, preferred_element_type=F32)
    lane = lax.broadcasted_iota(jnp.int32, (128, 128), 1)
    step = jnp.where((lane == 0) | (lane == 127), dt[...], 0.0)
    for v in range(5):
        @pl.loop(9 * v, 9 * v + 9, step=3)
        def _(first):
            for j in (first, first + 1, first + 2):
                turned = pltpu.roll(terms, 127 - 2 * j, 1)
                out[j] = acc[j] - step * turned

        pltpu.make_async_copy(
            out.at[pl.ds(9 * v, 9)], out_hbm.at[pl.ds(9 * v, 9)], sem.at[v]
        ).start()
    for v in range(5):
        pltpu.make_async_copy(
            out.at[pl.ds(9 * v, 9)], out_hbm.at[pl.ds(9 * v, 9)], sem.at[v]
        ).wait()


def swap(x, mask):
    return lax.ppermute(x, BLK, [(i, i ^ mask) for i in range(64)])


def ring(order):
    pairs, begin = [], 0
    for length in order:
        pairs += [(begin + i, begin + (i + 1) % length) for i in range(length)]
        begin += length
    return pairs


def ring_swaps(order):
    right = ring(order)
    left = [(t, s) for s, t in right]

    def run(rim_l, rim_r):
        return lax.ppermute(rim_r, BLK, right), lax.ppermute(rim_l, BLK, left)

    return run


def sds(*shape, dtype=F32):
    return jax.ShapeDtypeStruct(shape, dtype)


def call(kernel, outs, in_specs, out_specs, scratch=(), limit=8, flops=0, aliases={}):
    return pl.pallas_call(
        kernel,
        out_shape=outs,
        in_specs=in_specs,
        out_specs=out_specs,
        scratch_shapes=list(scratch),
        input_output_aliases=aliases,
        cost_estimate=pl.CostEstimate(flops=flops, bytes_accessed=flops // 8, transcendentals=0),
        compiler_params=pltpu.CompilerParams(vmem_limit_bytes=limit << 20),
    )


def per_device(state, base, dt, row_map, lag, count, jac, dis, freq):
    shape = state.shape
    x = state.reshape(45, 128, 128)
    b = base.reshape(45, 128, 128)
    dt = dt.reshape(128, 128)
    jac = jac.transpose(0, 2, 1, 3)
    x, b, row_map, lag, count, dis, freq, jac = [
        pltpu.with_memory_space_constraint(a, pltpu.HBM)
        for a in (x, b, row_map, lag, count, dis, freq, jac)
    ]
    quarter, rim = sds(2, 16, 128), sds(45, 8, 128)
    padded, whole = VMEM((45, 240, 128), F32), VMEM((45, 128, 128), F32)
    dma = pltpu.SemaphoreType.DMA
    x_hbm = x
    f0, f1, f2, f3, faces, x = call(
        faces_kernel,
        [quarter] * 4 + [sds(8, 16, 128), padded],
        [hspec()],
        [vspec()] * 6,
        [dma((8,))],
    )(x)
    r = []
    for d, f in ((1, f1), (2, f2), (3, f3)):
        r.append(swap(f, QUAD[d]))
    order, rim_l, rim_r, edge, forward = call(
        leave_kernel,
        [sds(1, dtype=jnp.int32), rim, rim, sds(45, 16, 128), sds(96, 64)],
        [hspec()] * 2 + [vspec()],
        [sspec()] + [vspec()] * 4,
        [pltpu.SMEM((64,), jnp.int32), pltpu.SMEM((3,), jnp.int32), dma((2,))],
        flops=2000000,
    )(row_map, lag, x)
    from_span = lax.ppermute(edge, "span", [(0, 1), (1, 0)])
    modes = call(
        project_kernel, sds(2, 64, 128), [vspec()] * 5, vspec(), flops=1000000
    )(f0, *r, forward)
    from_left, from_right = lax.switch(
        order[0], [ring_swaps(lengths) for lengths in ORDERS], rim_l, rim_r
    )
    for n, mask in enumerate(HOPS):
        other = swap(modes, mask)
        if n < 3:
            modes = modes + other
    x, backward, mixing, coef = call(
        tables_kernel,
        [padded, sds(128, 64), sds(128, 128), sds(COEFS, 8, 128)],
        [hspec()] * 6,
        [vspec()] * 4,
        [
            pltpu.SMEM((64,), jnp.int32),
            pltpu.SMEM((2,), jnp.int32),
            pltpu.SMEM((3, 3), F32),
            pltpu.SMEM((3,), F32),
            pltpu.SMEM((3, 5, 3, 5), F32),
            dma((5,)),
            dma((8,)),
        ],
        flops=3000000,
    )(row_map, count, dis, freq, jac, x_hbm)
    acc, b = call(
        functools.partial(along_first_kernel, *ALONG[0]),
        [whole, whole],
        [vspec()] * 2 + [hspec()],
        [vspec()] * 2,
        [dma],
        flops=10000000,
    )(coef, x, b)
    for first, last in ALONG[1:]:
        acc = call(
            functools.partial(along_kernel, first, last),
            whole,
            [vspec()] * 3,
            vspec(),
            flops=3000000 * (last - first),
            aliases={2: 0},
        )(coef, x, acc)
    x = call(
        ghosts_kernel, padded, [vspec()] * 5, vspec(), flops=1000000, aliases={4: 0}
    )(coef, from_left, from_right, from_span, x)
    for first, last in ACROSS:
        acc = call(
            functools.partial(across_kernel, first, last),
            whole,
            [vspec()] * 5,
            vspec(),
            flops=5000000 * (last - first),
            aliases={4: 0},
        )(coef, x, dt, b, acc)
    g = call(
        evaluate_kernel, [quarter] * 4, [vspec()] * 3, [vspec()] * 4, flops=1000000
    )(modes, other, backward)
    h = []
    for d in (1, 2, 3):
        h.append(swap(g[d], QUAD[d]))
    out = call(
        finish_kernel,
        sds(45, 128, 128),
        [vspec()] * 8,
        hspec(),
        [VMEM((45, 128, 128), F32), VMEM((128, 128), F32), dma((5,))],
        flops=10000000,
    )(acc, g[0], *h, faces, mixing, dt)
    return out.reshape(shape)


def solution(mesh):
    finer = Mesh(
        mesh.devices.reshape(4, 2, 4, 2, mesh.shape["span"]),
        ("blk_0", "blk_1", "blk_2", "blk_3", "span"),
    )
    return jax.shard_map(
        per_device,
        mesh=finer,
        in_specs=(
            P(None, None, "span", BLK, None),
            P(None, None, "span", BLK, None),
            P("span", BLK, None),
            P(),
            P(),
            P(),
            P(),
            P(),
            P(),
        ),
        out_specs=P(None, None, "span", BLK, None),
        check_vma=False,
    )
```

```python
import functools
import math

import jax
import jax.numpy as jnp
from jax import lax
from jax.experimental import pallas as pl
from jax.experimental.pallas import tpu as pltpu
from jax.sharding import Mesh
from jax.sharding import PartitionSpec as P

BLK = ("blk_0", "blk_1", "blk_2", "blk_3")
ENDS = (
    ((0, 32), (2, 34), (31, 63), (29, 61)),
    ((0, 28), (2, 30), (35, 63), (33, 61)),
)
EXACT = lax.Precision.HIGHEST
VMEM = pltpu.VMEM
F32 = jnp.float32
QUAD = (0, 1, 8, 9)
HOPS = (16, 48, 2, 6)
DN = tuple(0.5 * math.cos(math.pi * n) / math.sin(math.pi * n / 9) for n in range(5) if n)


ALONG = ((0, 5), (5, 8))
ACROSS = ((0, 1), (1, 5), (5, 8))
CENTRE, WAVE, SPAN, LEFT, RIGHT, COEFS = 90, 91, 95, 97, 98, 99


def vspec():
    return pl.BlockSpec(memory_space=VMEM)


def hspec():
    return pl.BlockSpec(memory_space=pltpu.HBM)


def own_block():
    return (
        (lax.axis_index("blk_0") * 2 + lax.axis_index("blk_1")) * 4 + lax.axis_index("blk_2")
    ) * 2 + lax.axis_index("blk_3")


def own_quarter():
    return lax.axis_index("blk_1") * 2 + lax.axis_index("blk_3")


def lengths_of(order):
    n0 = jnp.where(order < 2, 2, jnp.where(order < 4, 33, 29))
    n1 = jnp.where(
        (order == 2) | (order == 4), 2, jnp.where((order == 0) | (order == 5), 33, 29)
    )
    return n0, n1


def place_in_row(order, block):
    n0, n1 = lengths_of(order)
    row = (block >= n0).astype(jnp.int32) + (block >= n0 + n1).astype(jnp.int32)
    begin = jnp.where(row == 0, 0, jnp.where(row == 1, n0, n0 + n1))
    total = jnp.where(row == 0, n0, jnp.where(row == 1, n1, 64 - n0 - n1))
    return row, block - begin, total


def sine_and_cosine(count, period):
    inverse = 1.0 / period
    rest = count - jnp.floor(count * inverse + 0.5) * period
    quarters = rest * (4.0 * inverse)
    turn = jnp.floor(quarters + 0.5)
    z = (quarters - turn) * (0.5 * math.pi)
    y = z * z
    sin = z * (1.0 + y * (-1 / 6 + y * (1 / 120 + y * (-1 / 5040 + y * (1 / 362880)))))
    cos = 1.0 + y * (
        -1 / 2 + y * (1 / 24 + y * (-1 / 720 + y * (1 / 40320 + y * (-1 / 3628800))))
    )
    turn = turn.astype(jnp.int32) & 3
    odd = (turn & 1) == 1
    sin, cos = jnp.where(odd, cos, sin), jnp.where(odd, sin, cos)
    return jnp.where(turn >= 2, -sin, sin), jnp.where((turn == 1) | (turn == 2), -cos, cos)


def order_of(rows):
    late = rows[31] == 2
    first = jnp.where(rows[2] == 1, 0, jnp.where(rows[29] == 0, 2, 4))
    second = jnp.where(
        first == 0,
        late.astype(jnp.int32),
        jnp.where(first == 2, (rows[35] != 2).astype(jnp.int32), 1 - late.astype(jnp.int32)),
    )
    return first + second


def waves(members):
    shape = (16, 128)
    lane = lax.broadcasted_iota(jnp.int32, shape, 1)
    mode = lax.broadcasted_iota(jnp.int32, shape, 0)
    member = (lane // 16) & 3

    def pick(n):
        values = [jnp.full(shape, m[n], jnp.int32) for m in members]
        return jnp.where(
            member < 2,
            jnp.where(member == 0, values[0], values[1]),
            jnp.where(member == 2, values[2], values[3]),
        )

    its_row = pick(0)
    period = (pick(2) * 32).astype(F32)
    odd = ((pick(1) * 16 + (lane & 15)) * 2 + 1).astype(F32)
    sin, cos = sine_and_cosine(mode.astype(F32) * odd, period)
    return its_row, lane, mode, period, cos, sin


def members_of(order):
    block = own_block()
    return [place_in_row(order, lax.bitwise_xor(block, m)) for m in QUAD]


def write_forward(its_waves, forward):
    its_row, _, mode, period, cos, sin = its_waves
    weight = jnp.where(mode == 0, 2.0, 4.0) / period
    for r in range(3):
        here = its_row == r
        forward[pl.ds(32 * r, 16), :] = jnp.where(here, cos * weight, 0.0)[:, :64]
        forward[pl.ds(32 * r + 16, 16), :] = jnp.where(here, sin * weight, 0.0)[:, :64]


def write_rest(block, members, its_waves, count, dis, freq, jac, backward, mixing, coef):
    row, position, total = members[0]
    far_end = jnp.where(total == 33, 2.0, 3.0)
    even = (block & 1) == 0
    to_next, to_last = jnp.where(even, 0.0, 1.0), jnp.where(even, 1.0, 0.0)
    before = jnp.where(position > 0, to_last, jnp.where(total == 2, to_next, far_end))
    after = jnp.where(position < total - 1, to_next, jnp.where(total == 2, to_last, far_end))
    its_row, lane, mode, _, cos, sin = its_waves
    seen = its_row - jnp.where(lane < 64, 1, 0)
    back = []
    for gap in range(2):
        kept = (seen == gap) & (mode < count[gap])
        back += [jnp.where(kept, cos, 0.0), jnp.where(kept, sin, 0.0)]
    backward[...] = jnp.concatenate(back, axis=0).T

    shape = (128, 128)
    source = lax.broadcasted_iota(jnp.int32, shape, 0)
    target = lax.broadcasted_iota(jnp.int32, shape, 1)

    def variable(ids):
        return sum((ids >= 18 * n).astype(jnp.int32) for n in range(1, 5))

    line = lax.broadcasted_iota(jnp.int32, (8, 128), 1)
    u_of = variable(line)
    v_of = variable(lax.broadcasted_iota(jnp.int32, (128, 1), 0))
    crossed = lax.bitwise_xor(target, 1)
    same = (crossed - 18 * u_of[:1]) == (source - 18 * v_of)
    terms = jnp.zeros(shape, F32)
    for v in range(5):
        entries = jnp.zeros((8, 128), F32)
        for u in range(5):
            entries = jnp.where(u_of == u, jac[row, u, 1, v], entries)
        terms = jnp.where(v_of == v, entries[:1], terms)
    terms = terms * jnp.where((source & 1) == 0, -0.5, 0.5)
    terms = terms - jnp.where(crossed == source, dis[row, 1], 0.0)
    mixing[...] = jnp.where(same & (source < 90), terms, 0.0)

    def put(at, value):
        coef[at] = jnp.full((8, 128), value, F32)

    for d in range(3):
        for u in range(5):
            for v in range(5):
                half = 0.5 * jac[row, u, d, v]
                if u == v:
                    put(75 + d * 5 + u, half - dis[row, d])
                    put(d * 25 + u * 5 + v, half + dis[row, d])
                else:
                    put(d * 25 + u * 5 + v, half)
    put(CENTRE, 2.0 * (dis[row, 0] + dis[row, 1] + dis[row, 2]))
    for n in range(4):
        put(WAVE + n, freq[row] * DN[n])
    upper = lax.axis_index("span")
    put(LEFT, before)
    put(RIGHT, after)
    put(SPAN, upper.astype(F32))
    put(SPAN + 1, (1 - upper).astype(F32))


def faces_kernel(x_hbm, kept, sent, faces, x, sem):
    copies = [
        pltpu.make_async_copy(
            x_hbm.at[:, pl.ds(16 * s, 16), :], x.at[:, pl.ds(24 * s + 32, 16), :], sem.at[s]
        )
        for s in range(8)
    ]
    for copy in copies:
        copy.start()
    lane = lax.broadcasted_iota(jnp.int32, (8, 128), 1) // 2
    for s in range(8):
        copies[s].wait()
        acc = [jnp.zeros((8, 128), F32) for _ in range(2)]
        for j in range(45):
            for h in range(2):
                turned = pltpu.roll(x[j, pl.ds(24 * s + 32 + 8 * h, 8), :], 2 * j + 1, 1)
                acc[h] = jnp.where(lane == j, turned, acc[h])
        for h in range(2):
            faces[s, pl.ds(8 * h, 8), :] = acc[h]
    core = lax.axis_index("blk_3")
    for y in range(2):
        kept[y] = faces[pl.ds(4 * y + 2 * core, 2)]
        sent[y] = faces[pl.ds(4 * y + 2 - 2 * core, 2)]


def pair_kernel(kept, other, sent):
    y = 1 - lax.axis_index("blk_1")
    sent[0] = kept[y]
    sent[1] = other[y]


def pack_kernel(first, second, sent):
    sent[0] = first[...]
    sent[1] = second[1]


def leave_kernel(
    rows_hbm, lag_hbm, count_hbm, dis_hbm, freq_hbm, jac_hbm, dt_hbm, x,
    rims, rim_w, edge, forward, backward, mixing, coef, dt,
    rows, lag, count, dis, freq, jac, sem,
):
    small = [
        pltpu.make_async_copy(a, b, sem.at[n])
        for n, (a, b) in enumerate(
            (
                (rows_hbm, rows), (lag_hbm, lag), (count_hbm, count),
                (dis_hbm, dis), (freq_hbm, freq), (jac_hbm, jac), (dt_hbm, dt),
            )
        )
    ]
    for copy in small:
        copy.start()
    outer = pl.multiple_of(jnp.where(lax.axis_index("span") == 0, 200, 32), 8)

    @pl.loop(0, 9)
    def _(k):
        for v in range(5):
            edge[v * 9 + k] = x[v * 9 + k, pl.ds(outer, 16), :]

    for copy in small:
        copy.wait()
    members = members_of(order_of(rows))
    its_waves = waves(members)
    write_forward(its_waves, forward)
    write_rest(own_block(), members, its_waves, count, dis, freq, jac, backward, mixing, coef)
    row, position, total = members[0]
    at_begin, at_final = position == 0, position == total - 1
    turn = jnp.where(at_begin, 9 - lag[row], lag[row])
    end = jnp.where(at_begin, 32, 47)
    turn_left = jnp.where(at_begin & (total == 2), turn, 0)
    turn_right = jnp.where(at_final & (total == 2), turn, 0)

    @pl.loop(0, 9)
    def _(k):
        for v in range(5):
            j = v * 9 + k
            rims[j] = x[v * 9 + lax.rem(k + turn_left, 9), pl.ds(32, 8, stride=24), :]
            rims[45 + j] = x[v * 9 + lax.rem(k + turn_right, 9), pl.ds(47, 8, stride=24), :]
            rim_w[j] = x[v * 9 + lax.rem(k + turn, 9), pl.ds(end, 8, stride=24), :]


def project_kernel(kept, other, far, forward, out):
    y = lax.axis_index("blk_1")
    even = lax.broadcasted_iota(jnp.int32, (32, 128), 1) % 2 == 0
    for i in range(2):
        columns = jnp.concatenate([kept[y, i], other[y, i], far[0, i], far[1, i]], axis=0)
        parts = jnp.dot(forward[...], columns, precision=EXACT, preferred_element_type=F32)
        low, mid, high = parts[:32], parts[32:64], parts[64:]
        out[i, pl.ds(0, 32), :] = jnp.where(even, low, mid)
        out[i, pl.ds(32, 32), :] = jnp.where(even, mid, high)


def evaluate_kernel(m0, m1, backward, own, core, far):
    even = lax.broadcasted_iota(jnp.int32, (64, 128), 1) % 2 == 0
    for i in range(2):
        modes = m0[i] + m1[i]
        both = jnp.dot(backward[...], modes, precision=EXACT, preferred_element_type=F32)
        ghost = jnp.where(even, both[:64], both[64:])
        own[i] = ghost[:16]
        core[i] = ghost[16:32]
        far[0, i] = ghost[32:48]
        far[1, i] = ghost[48:]


def ghosts_kernel(coef, core, chip, wrap0, wrap1, edge, x_in, x):
    left, right = coef[LEFT], coef[RIGHT]
    keep_low = jnp.concatenate([coef[SPAN]] * 2, axis=0)
    keep_high = jnp.concatenate([coef[SPAN + 1]] * 2, axis=0)

    @pl.loop(0, 9)
    def _(k):
        for v in range(5):
            j = v * 9 + k
            low, high = core[45 + j], core[j]
            low = jnp.where(left == 1, chip[45 + j], low)
            high = jnp.where(right == 1, chip[j], high)
            for w, wrap in ((2, wrap0), (3, wrap1)):
                low = jnp.where(left == w, wrap[j], low)
                high = jnp.where(right == w, wrap[j], high)
            x[j, pl.ds(31, 8, stride=24), :] = low
            x[j, pl.ds(48, 8, stride=24), :] = high
            x[j, pl.ds(8, 16), :] = edge[j] * keep_low
            x[j, pl.ds(224, 16), :] = edge[j] * keep_high


def across_kernel(first, last, coef, x, dt, base, out_in, out):
    @pl.loop(first, last)
    def _(s):
        at = pl.multiple_of(24 * s + 32, 8)
        to = pl.multiple_of(16 * s, 16)
        for h in range(2):
            there = pl.ds(to + 8 * h, 8)
            step = dt[there, :]
            for k in range(9):
                acc, diffs = [], []
                for v in range(5):
                    j = v * 9 + k
                    pairs = [
                        (d, x[j, pl.ds(at + 8 * h + r, 8), :], x[j, pl.ds(at + 8 * h - r, 8), :])
                        for d, r in ((0, 1), (2, 24))
                    ]
                    diffs.append({d: plus - minus for d, plus, minus in pairs})
                    terms = [
                        plus * coef[75 + d * 5 + v] - minus * coef[d * 25 + v * 6]
                        for d, plus, minus in pairs
                    ]
                    acc.append(terms[0] + terms[1])
                for u in range(5):
                    j = u * 9 + k
                    total_u = out[j, there, :] + acc[u]
                    for d in (0, 2):
                        part = None
                        for v in range(5):
                            if v != u:
                                product = diffs[v][d] * coef[d * 25 + u * 5 + v]
                                part = product if part is None else part + product
                        total_u = total_u + part
                    out[j, there, :] = base[j, there, :] - step * total_u


def along_first_kernel(first, last, coef, x, base_hbm, out, base, sem):
    fetch = pltpu.make_async_copy(base_hbm, base, sem)
    fetch.start()
    along_kernel(first, last, coef, x, out)
    fetch.wait()


def along_kernel(first, last, coef, x, *refs):
    out = refs[-1]

    @pl.loop(first, last)
    def _(s):
        at = pl.multiple_of(24 * s + 32, 8)
        to = pl.multiple_of(16 * s, 16)
        for h in range(2):
            here, there = pl.ds(at + 8 * h, 8), pl.ds(to + 8 * h, 8)
            for u in range(5):
                line = [x[u * 9 + k, here, :] for k in range(9)]
                for k in range(9):
                    turn = [
                        (line[(k - n) % 9] - line[(k + n) % 9]) * coef[WAVE + n - 1]
                        for n in range(1, 5)
                    ]
                    turn.append(line[k] * coef[CENTRE])
                    out[u * 9 + k, there, :] = (turn[0] + turn[1]) + (turn[2] + turn[3]) + turn[4]
            for k in range(9):
                acc, diffs = [], []
                for v in range(5):
                    j = v * 9 + k
                    own = x[j, here, :]
                    plus, minus = pltpu.roll(own, 127, 1), pltpu.roll(own, 1, 1)
                    diffs.append(plus - minus)
                    acc.append(
                        out[j, there, :]
                        + (plus * coef[80 + v] - minus * coef[25 + v * 6])
                    )
                for u in range(5):
                    part = None
                    for v in range(5):
                        if v != u:
                            product = diffs[v] * coef[25 + u * 5 + v]
                            part = product if part is None else part + product
                    out[u * 9 + k, there, :] = acc[u] + part


def finish_kernel(acc, own, core, far, faces, mixing, dt, out_hbm, out, ghost, sem):
    q = own_quarter()
    for d, ref in enumerate((own, core.at[0], far.at[0], core.at[1])):
        for i in range(2):
            s = 2 * lax.bitwise_xor(q, d) + i
            ghost[pl.ds(pl.multiple_of(16 * s, 16), 16), :] = ref[i] - faces[s]
    terms = jnp.dot(ghost[...], mixing[...], precision=EXACT, preferred_element_type=F32)
    lane = lax.broadcasted_iota(jnp.int32, (128, 128), 1)
    step = jnp.where((lane == 0) | (lane == 127), dt[...], 0.0)
    for v in range(5):
        @pl.loop(9 * v, 9 * v + 9, step=3)
        def _(first):
            for j in (first, first + 1, first + 2):
                turned = pltpu.roll(terms, 127 - 2 * j, 1)
                out[j] = acc[j] - step * turned

        pltpu.make_async_copy(
            out.at[pl.ds(9 * v, 9)], out_hbm.at[pl.ds(9 * v, 9)], sem.at[v]
        ).start()
    for v in range(5):
        pltpu.make_async_copy(
            out.at[pl.ds(9 * v, 9)], out_hbm.at[pl.ds(9 * v, 9)], sem.at[v]
        ).wait()


def swap(x, mask):
    return lax.ppermute(x, BLK, [(i, i ^ mask) for i in range(64)])


def other_end(x, pairs):
    ends = dict(pairs) | {b: a for a, b in pairs}
    return lax.ppermute(x, BLK, [(i, ends.get(i, i)) for i in range(64)])


def sds(*shape, dtype=F32):
    return jax.ShapeDtypeStruct(shape, dtype)


def call(kernel, outs, in_specs, out_specs, scratch=(), limit=8, flops=0, aliases={}):
    return pl.pallas_call(
        kernel,
        out_shape=outs,
        in_specs=in_specs,
        out_specs=out_specs,
        scratch_shapes=list(scratch),
        input_output_aliases=aliases,
        cost_estimate=pl.CostEstimate(flops=flops, bytes_accessed=flops // 8, transcendentals=0),
        compiler_params=pltpu.CompilerParams(vmem_limit_bytes=limit << 20),
    )


def per_device(state, base, dt, row_map, lag, count, jac, dis, freq):
    shape = state.shape
    x = state.reshape(45, 128, 128)
    b = base.reshape(45, 128, 128)
    dt = dt.reshape(128, 128)
    jac = jac.transpose(0, 2, 1, 3)
    x, b, dt, row_map, lag, count, dis, freq, jac = [
        pltpu.with_memory_space_constraint(a, pltpu.HBM)
        for a in (x, b, dt, row_map, lag, count, dis, freq, jac)
    ]
    quarter, rim = sds(2, 16, 128), sds(45, 8, 128)
    padded, whole = VMEM((45, 240, 128), F32), VMEM((45, 128, 128), F32)
    dma = pltpu.SemaphoreType.DMA
    pair = sds(2, 2, 16, 128)
    kept, sent, faces, x = call(
        faces_kernel, [pair, pair, sds(8, 16, 128), padded], [hspec()], [vspec()] * 4, [dma((8,))]
    )(x)
    other = swap(sent, 1)
    sent = call(pair_kernel, pair, [vspec()] * 2, vspec())(kept, other)
    far = swap(sent, 8)
    rims, rim_w, edge, forward, backward, mixing, coef, dt = call(
        leave_kernel,
        [sds(90, 8, 128), rim, sds(45, 16, 128), sds(96, 64)]
        + [sds(128, 64), sds(128, 128), sds(COEFS, 8, 128), sds(128, 128)],
        [hspec()] * 7 + [vspec()],
        [vspec()] * 8,
        [
            pltpu.SMEM((64,), jnp.int32),
            pltpu.SMEM((3,), jnp.int32),
            pltpu.SMEM((2,), jnp.int32),
            pltpu.SMEM((3, 3), F32),
            pltpu.SMEM((3,), F32),
            pltpu.SMEM((3, 5, 3, 5), F32),
            dma((7,)),
        ],
        flops=2000000,
    )(row_map, lag, count, dis, freq, jac, dt, x)
    from_span = lax.ppermute(edge, "span", [(0, 1), (1, 0)])
    modes = call(
        project_kernel, sds(2, 64, 128), [vspec()] * 4, vspec(), flops=1000000
    )(kept, other, far, forward)
    from_core = swap(rims, 1)
    from_chip = other_end(rims, [(i, i + 1) for i in range(1, 63, 2)])
    wraps = []
    for pairs in ENDS:
        wraps.append(other_end(rim_w, pairs))
    for n, mask in enumerate(HOPS):
        other = swap(modes, mask)
        if n < 3:
            modes = modes + other
    acc, b = call(
        functools.partial(along_first_kernel, *ALONG[0]),
        [whole, whole],
        [vspec()] * 2 + [hspec()],
        [vspec()] * 2,
        [dma],
        flops=10000000,
    )(coef, x, b)
    for first, last in ALONG[1:]:
        acc = call(
            functools.partial(along_kernel, first, last),
            whole,
            [vspec()] * 3,
            vspec(),
            flops=3000000 * (last - first),
            aliases={2: 0},
        )(coef, x, acc)
    x = call(
        ghosts_kernel, padded, [vspec()] * 7, vspec(), flops=1000000, aliases={6: 0}
    )(coef, from_core, from_chip, *wraps, from_span, x)
    for first, last in ACROSS:
        acc = call(
            functools.partial(across_kernel, first, last),
            whole,
            [vspec()] * 5,
            vspec(),
            flops=5000000 * (last - first),
            aliases={4: 0},
        )(coef, x, dt, b, acc)
    own, core, far = call(
        evaluate_kernel, [quarter, quarter, pair], [vspec()] * 3, [vspec()] * 3, flops=1000000
    )(modes, other, backward)
    far = swap(far, 8)
    core = call(pack_kernel, pair, [vspec()] * 2, vspec())(core, far)
    core = swap(core, 1)
    out = call(
        finish_kernel,
        sds(45, 128, 128),
        [vspec()] * 7,
        hspec(),
        [VMEM((45, 128, 128), F32), VMEM((128, 128), F32), dma((5,))],
        flops=10000000,
    )(acc, own, core, far, faces, mixing, dt)
    return out.reshape(shape)


def solution(mesh):
    finer = Mesh(
        mesh.devices.reshape(4, 2, 4, 2, mesh.shape["span"]),
        ("blk_0", "blk_1", "blk_2", "blk_3", "span"),
    )
    return jax.shard_map(
        per_device,
        mesh=finer,
        in_specs=(
            P(None, None, "span", BLK, None),
            P(None, None, "span", BLK, None),
            P("span", BLK, None),
            P(),
            P(),
            P(),
            P(),
            P(),
            P(),
        ),
        out_specs=P(None, None, "span", BLK, None),
        check_vma=False,
    )
```

```python
import functools
import math

import jax
import jax.numpy as jnp
from jax import lax
from jax.experimental import pallas as pl
from jax.experimental.pallas import tpu as pltpu
from jax.sharding import Mesh
from jax.sharding import PartitionSpec as P

BLK = ("blk_0", "blk_1", "blk_2", "blk_3")
ENDS = (
    ((0, 32), (2, 34), (31, 63), (29, 61)),
    ((0, 28), (2, 30), (35, 63), (33, 61)),
)
EXACT = lax.Precision.HIGHEST
VMEM = pltpu.VMEM
F32 = jnp.float32
QUAD = (0, 1, 8, 9)
HOPS = (16, 48, 2, 6)
DN = tuple(0.5 * math.cos(math.pi * n) / math.sin(math.pi * n / 9) for n in range(5) if n)


ALONG = ((0, 5), (5, 8))
ACROSS = ((0, 3), (3, 7))
LAST = (7, 8)
CENTRE, WAVE, SPAN, LEFT, RIGHT, COEFS = 90, 91, 95, 97, 98, 99


def vspec():
    return pl.BlockSpec(memory_space=VMEM)


def hspec():
    return pl.BlockSpec(memory_space=pltpu.HBM)


def own_block():
    return (
        (lax.axis_index("blk_0") * 2 + lax.axis_index("blk_1")) * 4 + lax.axis_index("blk_2")
    ) * 2 + lax.axis_index("blk_3")


def lengths_of(order):
    n0 = jnp.where(order < 2, 2, jnp.where(order < 4, 33, 29))
    n1 = jnp.where(
        (order == 2) | (order == 4), 2, jnp.where((order == 0) | (order == 5), 33, 29)
    )
    return n0, n1


def place_in_row(order, block):
    n0, n1 = lengths_of(order)
    row = (block >= n0).astype(jnp.int32) + (block >= n0 + n1).astype(jnp.int32)
    begin = jnp.where(row == 0, 0, jnp.where(row == 1, n0, n0 + n1))
    total = jnp.where(row == 0, n0, jnp.where(row == 1, n1, 64 - n0 - n1))
    return row, block - begin, total


def sine_and_cosine(count, period):
    inverse = 1.0 / period
    rest = count - jnp.floor(count * inverse + 0.5) * period
    quarters = rest * (4.0 * inverse)
    turn = jnp.floor(quarters + 0.5)
    z = (quarters - turn) * (0.5 * math.pi)
    y = z * z
    sin = z * (1.0 + y * (-1 / 6 + y * (1 / 120 + y * (-1 / 5040 + y * (1 / 362880)))))
    cos = 1.0 + y * (
        -1 / 2 + y * (1 / 24 + y * (-1 / 720 + y * (1 / 40320 + y * (-1 / 3628800))))
    )
    turn = turn.astype(jnp.int32) & 3
    odd = (turn & 1) == 1
    sin, cos = jnp.where(odd, cos, sin), jnp.where(odd, sin, cos)
    return jnp.where(turn >= 2, -sin, sin), jnp.where((turn == 1) | (turn == 2), -cos, cos)


def order_of(rows):
    late = rows[31] == 2
    first = jnp.where(rows[2] == 1, 0, jnp.where(rows[29] == 0, 2, 4))
    second = jnp.where(
        first == 0,
        late.astype(jnp.int32),
        jnp.where(first == 2, (rows[35] != 2).astype(jnp.int32), 1 - late.astype(jnp.int32)),
    )
    return first + second


def waves(members):
    shape = (16, 128)
    lane = lax.broadcasted_iota(jnp.int32, shape, 1)
    mode = lax.broadcasted_iota(jnp.int32, shape, 0)
    member = (lane // 16) & 3

    def pick(n):
        values = [jnp.full(shape, m[n], jnp.int32) for m in members]
        return jnp.where(
            member < 2,
            jnp.where(member == 0, values[0], values[1]),
            jnp.where(member == 2, values[2], values[3]),
        )

    its_row = pick(0)
    period = (pick(2) * 32).astype(F32)
    odd = ((pick(1) * 16 + (lane & 15)) * 2 + 1).astype(F32)
    sin, cos = sine_and_cosine(mode.astype(F32) * odd, period)
    return its_row, lane, mode, period, cos, sin


def members_of(order):
    block = own_block()
    return [place_in_row(order, lax.bitwise_xor(block, m)) for m in QUAD]


def write_forward(its_waves, forward):
    its_row, _, mode, period, cos, sin = its_waves
    weight = jnp.where(mode == 0, 2.0, 4.0) / period
    for r in range(3):
        here = its_row == r
        forward[pl.ds(32 * r, 16), :] = jnp.where(here, cos * weight, 0.0)[:, :64]
        forward[pl.ds(32 * r + 16, 16), :] = jnp.where(here, sin * weight, 0.0)[:, :64]


def write_rest(block, members, its_waves, count, dis, freq, jac, backward, mixing, coef):
    row, position, total = members[0]
    far_end = jnp.where(total == 33, 2.0, 3.0)
    even = (block & 1) == 0
    to_next, to_last = jnp.where(even, 0.0, 1.0), jnp.where(even, 1.0, 0.0)
    before = jnp.where(position > 0, to_last, jnp.where(total == 2, to_next, far_end))
    after = jnp.where(position < total - 1, to_next, jnp.where(total == 2, to_last, far_end))
    its_row, lane, mode, _, cos, sin = its_waves
    seen = its_row - jnp.where(lane < 64, 1, 0)
    back = []
    for gap in range(2):
        kept = (seen == gap) & (mode < count[gap])
        back += [jnp.where(kept, cos, 0.0), jnp.where(kept, sin, 0.0)]
    backward[...] = jnp.concatenate(back, axis=0).T

    shape = (128, 128)
    source = lax.broadcasted_iota(jnp.int32, shape, 0)
    target = lax.broadcasted_iota(jnp.int32, shape, 1)

    def variable(ids):
        return sum((ids >= 18 * n).astype(jnp.int32) for n in range(1, 5))

    line = lax.broadcasted_iota(jnp.int32, (8, 128), 1)
    u_of = variable(line)
    v_of = variable(lax.broadcasted_iota(jnp.int32, (128, 1), 0))
    crossed = lax.bitwise_xor(target, 1)
    same = (crossed - 18 * u_of[:1]) == (source - 18 * v_of)
    terms = jnp.zeros(shape, F32)
    for v in range(5):
        entries = jnp.zeros((8, 128), F32)
        for u in range(5):
            entries = jnp.where(u_of == u, jac[row, u, 1, v], entries)
        terms = jnp.where(v_of == v, entries[:1], terms)
    terms = terms * jnp.where((source & 1) == 0, -0.5, 0.5)
    terms = terms - jnp.where(crossed == source, dis[row, 1], 0.0)
    mixing[...] = jnp.where(same & (source < 90), terms, 0.0)

    def put(at, value):
        coef[at] = jnp.full((8, 128), value, F32)

    for d in range(3):
        for u in range(5):
            for v in range(5):
                half = 0.5 * jac[row, u, d, v]
                if u == v:
                    put(75 + d * 5 + u, half - dis[row, d])
                    put(d * 25 + u * 5 + v, half + dis[row, d])
                else:
                    put(d * 25 + u * 5 + v, half)
    put(CENTRE, 2.0 * (dis[row, 0] + dis[row, 1] + dis[row, 2]))
    for n in range(4):
        put(WAVE + n, freq[row] * DN[n])
    upper = lax.axis_index("span")
    put(LEFT, before)
    put(RIGHT, after)
    put(SPAN, upper.astype(F32))
    put(SPAN + 1, (1 - upper).astype(F32))


def faces_kernel(x_hbm, kept, sent, faces, x, sem):
    copies = [
        pltpu.make_async_copy(
            x_hbm.at[:, pl.ds(16 * s, 16), :], x.at[:, pl.ds(24 * s + 32, 16), :], sem.at[s]
        )
        for s in range(8)
    ]
    for copy in copies:
        copy.start()
    lane = lax.broadcasted_iota(jnp.int32, (8, 128), 1) // 2
    for s in range(8):
        copies[s].wait()
        acc = [jnp.zeros((8, 128), F32) for _ in range(2)]
        for j in range(45):
            for h in range(2):
                turned = pltpu.roll(x[j, pl.ds(24 * s + 32 + 8 * h, 8), :], 2 * j + 1, 1)
                acc[h] = jnp.where(lane == j, turned, acc[h])
        for h in range(2):
            faces[s, pl.ds(8 * h, 8), :] = acc[h]
    core = lax.axis_index("blk_3")
    for y in range(2):
        kept[y] = faces[pl.ds(4 * y + 2 * core, 2)]
        sent[y] = faces[pl.ds(4 * y + 2 - 2 * core, 2)]


def pair_kernel(kept, other, sent):
    y = 1 - lax.axis_index("blk_1")
    sent[0] = kept[y]
    sent[1] = other[y]


def pack_kernel(first, second, sent):
    sent[0] = first[...]
    sent[1] = second[1]


def leave_kernel(
    rows_hbm, lag_hbm, count_hbm, dis_hbm, freq_hbm, jac_hbm, dt_hbm, x,
    rims, rim_w, edge, forward, backward, mixing, coef, dt,
    rows, lag, count, dis, freq, jac, sem,
):
    small = [
        pltpu.make_async_copy(a, b, sem.at[n])
        for n, (a, b) in enumerate(
            (
                (rows_hbm, rows), (lag_hbm, lag), (count_hbm, count),
                (dis_hbm, dis), (freq_hbm, freq), (jac_hbm, jac), (dt_hbm, dt),
            )
        )
    ]
    for copy in small:
        copy.start()
    outer = pl.multiple_of(jnp.where(lax.axis_index("span") == 0, 200, 32), 8)

    @pl.loop(0, 9)
    def _(k):
        for v in range(5):
            edge[v * 9 + k] = x[v * 9 + k, pl.ds(outer, 16), :]

    for copy in small:
        copy.wait()
    members = members_of(order_of(rows))
    its_waves = waves(members)
    write_forward(its_waves, forward)
    write_rest(own_block(), members, its_waves, count, dis, freq, jac, backward, mixing, coef)
    row, position, total = members[0]
    at_begin, at_final = position == 0, position == total - 1
    turn = jnp.where(at_begin, 9 - lag[row], lag[row])
    end = jnp.where(at_begin, 32, 47)
    turn_left = jnp.where(at_begin & (total == 2), turn, 0)
    turn_right = jnp.where(at_final & (total == 2), turn, 0)

    @pl.loop(0, 9)
    def _(k):
        for v in range(5):
            j = v * 9 + k
            rims[j] = x[v * 9 + lax.rem(k + turn_left, 9), pl.ds(32, 8, stride=24), :]
            rims[45 + j] = x[v * 9 + lax.rem(k + turn_right, 9), pl.ds(47, 8, stride=24), :]
            rim_w[j] = x[v * 9 + lax.rem(k + turn, 9), pl.ds(end, 8, stride=24), :]


def project_kernel(kept, other, far, forward, out):
    y = lax.axis_index("blk_1")
    even = lax.broadcasted_iota(jnp.int32, (32, 128), 1) % 2 == 0
    for i in range(2):
        columns = jnp.concatenate([kept[y, i], other[y, i], far[0, i], far[1, i]], axis=0)
        parts = jnp.dot(forward[...], columns, precision=EXACT, preferred_element_type=F32)
        low, mid, high = parts[:32], parts[32:64], parts[64:]
        out[i, pl.ds(0, 32), :] = jnp.where(even, low, mid)
        out[i, pl.ds(32, 32), :] = jnp.where(even, mid, high)


def evaluate_kernel(m0, m1, backward, own, core, far):
    even = lax.broadcasted_iota(jnp.int32, (64, 128), 1) % 2 == 0
    for i in range(2):
        modes = m0[i] + m1[i]
        both = jnp.dot(backward[...], modes, precision=EXACT, preferred_element_type=F32)
        ghost = jnp.where(even, both[:64], both[64:])
        own[i] = ghost[:16]
        core[i] = ghost[16:32]
        far[0, i] = ghost[32:48]
        far[1, i] = ghost[48:]


def cells_of(place):
    core = lax.axis_index("blk_3")
    return 2 * jnp.where(place < 4, core, 1 - core) + (place & 1) + 4 * ((place >> 1) & 1)


def ghosts_kernel(coef, core, chip, wrap0, wrap1, edge, x_in, x):
    left, right = coef[LEFT], coef[RIGHT]
    keep_low = jnp.concatenate([coef[SPAN]] * 2, axis=0)
    keep_high = jnp.concatenate([coef[SPAN + 1]] * 2, axis=0)

    @pl.loop(0, 9)
    def _(k):
        for v in range(5):
            j = v * 9 + k
            low, high = core[45 + j], core[j]
            low = jnp.where(left == 1, chip[45 + j], low)
            high = jnp.where(right == 1, chip[j], high)
            for w, wrap in ((2, wrap0), (3, wrap1)):
                low = jnp.where(left == w, wrap[j], low)
                high = jnp.where(right == w, wrap[j], high)
            x[j, pl.ds(31, 8, stride=24), :] = low
            x[j, pl.ds(48, 8, stride=24), :] = high
            x[j, pl.ds(8, 16), :] = edge[j] * keep_low
            x[j, pl.ds(224, 16), :] = edge[j] * keep_high


def across_kernel(first, last, coef, x, dt, base, out_in, out):
    @pl.loop(first, last)
    def _(place):
        s = cells_of(place)
        at = pl.multiple_of(24 * s + 32, 8)
        to = pl.multiple_of(16 * s, 16)
        for h in range(2):
            there = pl.ds(to + 8 * h, 8)
            step = dt[there, :]
            for k in range(9):
                acc, diffs = [], []
                for v in range(5):
                    j = v * 9 + k
                    pairs = [
                        (d, x[j, pl.ds(at + 8 * h + r, 8), :], x[j, pl.ds(at + 8 * h - r, 8), :])
                        for d, r in ((0, 1), (2, 24))
                    ]
                    diffs.append({d: plus - minus for d, plus, minus in pairs})
                    terms = [
                        plus * coef[75 + d * 5 + v] - minus * coef[d * 25 + v * 6]
                        for d, plus, minus in pairs
                    ]
                    acc.append(terms[0] + terms[1])
                for u in range(5):
                    j = u * 9 + k
                    total_u = out[j, there, :] + acc[u]
                    for d in (0, 2):
                        part = None
                        for v in range(5):
                            if v != u:
                                product = diffs[v][d] * coef[d * 25 + u * 5 + v]
                                part = product if part is None else part + product
                        total_u = total_u + part
                    out[j, there, :] = base[j, there, :] - step * total_u


def along_first_kernel(first, last, coef, x, base_hbm, out, base, sem):
    fetch = pltpu.make_async_copy(base_hbm, base, sem)
    fetch.start()
    along_kernel(first, last, coef, x, out)
    fetch.wait()


def along_kernel(first, last, coef, x, *refs):
    out = refs[-1]

    @pl.loop(first, last)
    def _(s):
        at = pl.multiple_of(24 * s + 32, 8)
        to = pl.multiple_of(16 * s, 16)
        for h in range(2):
            here, there = pl.ds(at + 8 * h, 8), pl.ds(to + 8 * h, 8)
            for u in range(5):
                line = [x[u * 9 + k, here, :] for k in range(9)]
                for k in range(9):
                    turn = [
                        (line[(k - n) % 9] - line[(k + n) % 9]) * coef[WAVE + n - 1]
                        for n in range(1, 5)
                    ]
                    turn.append(line[k] * coef[CENTRE])
                    out[u * 9 + k, there, :] = (turn[0] + turn[1]) + (turn[2] + turn[3]) + turn[4]
            for k in range(9):
                acc, diffs = [], []
                for v in range(5):
                    j = v * 9 + k
                    own = x[j, here, :]
                    plus, minus = pltpu.roll(own, 127, 1), pltpu.roll(own, 1, 1)
                    diffs.append(plus - minus)
                    acc.append(
                        out[j, there, :]
                        + (plus * coef[80 + v] - minus * coef[25 + v * 6])
                    )
                for u in range(5):
                    part = None
                    for v in range(5):
                        if v != u:
                            product = diffs[v] * coef[25 + u * 5 + v]
                            part = product if part is None else part + product
                    out[u * 9 + k, there, :] = acc[u] + part


def add_ghosts(places, refs, faces, mixing, dt, acc, stage, ghost, after):
    cells = [cells_of(p) for p in places]
    for n, (s, ref) in enumerate(zip(cells, refs)):
        ghost[pl.ds(16 * n, 16), :] = ref[...] - faces[s]
    terms = jnp.dot(ghost[...], mixing[...], precision=EXACT, preferred_element_type=F32)
    lane = lax.broadcasted_iota(jnp.int32, (16, 128), 1)
    rows = [pl.ds(pl.multiple_of(16 * s, 16), 16) for s in cells]
    steps = [jnp.where((lane == 0) | (lane == 127), dt[r, :], 0.0) for r in rows]
    for v in range(5):
        for j in range(9 * v, 9 * v + 9):
            turned = pltpu.roll(terms, 127 - 2 * j, 1)
            for n in range(4):
                stage[j, pl.ds(16 * n, 16), :] = (
                    acc[j, rows[n], :] - steps[n] * turned[16 * n : 16 * n + 16]
                )

        after(v)


def writes(stage, out_hbm, sem, first, variables):
    core = lax.axis_index("blk_3")
    core = core if first else 1 - core
    lines = pl.ds(9 * variables[0], 9 * len(variables))
    return [
        pltpu.make_async_copy(
            stage.at[lines, pl.ds(32 * n, 32), :],
            out_hbm.at[lines, pl.ds(pl.multiple_of(32 * core + 64 * n, 32), 32), :],
            sem.at[variables[0], n],
        )
        for n in range(2)
    ]


def near_kernel(
    first, last, coef, x, dt, base, acc_in, own, far, faces, mixing,
    acc, out_hbm, stage, ghost, sem,
):
    def send(v):
        for copy in writes(stage, out_hbm, sem, True, (v,)):
            copy.start()

    refs = []
    for half in range(2):
        mine = (lax.axis_index("blk_1") == half)
        for i in range(2):
            refs.append(jnp.where(mine, own[i], far[0, i]))
    add_ghosts(range(4), refs, faces, mixing, dt, acc, stage, ghost, send)
    across_kernel(first, last, coef, x, dt, base, None, acc)
    for v in range(5):
        for copy in writes(stage, out_hbm, sem, True, (v,)):
            copy.wait()


def finish_kernel(acc, core, faces, mixing, dt, out_in, out_hbm, stage, ghost, sem):
    def send(v):
        for copy in writes(stage, out_hbm, sem, False, (v,)):
            copy.start()

    refs = []
    for half in range(2):
        mine = (lax.axis_index("blk_1") == half)
        for i in range(2):
            refs.append(jnp.where(mine, core[0, i], core[1, i]))
    add_ghosts(range(4, 8), refs, faces, mixing, dt, acc, stage, ghost, send)
    for v in range(5):
        for copy in writes(stage, out_hbm, sem, False, (v,)):
            copy.wait()


def swap(x, mask):
    return lax.ppermute(x, BLK, [(i, i ^ mask) for i in range(64)])


def other_end(x, pairs):
    ends = dict(pairs) | {b: a for a, b in pairs}
    return lax.ppermute(x, BLK, [(i, ends.get(i, i)) for i in range(64)])


def sds(*shape, dtype=F32):
    return jax.ShapeDtypeStruct(shape, dtype)


def call(kernel, outs, in_specs, out_specs, scratch=(), limit=8, flops=0, aliases={}):
    return pl.pallas_call(
        kernel,
        out_shape=outs,
        in_specs=in_specs,
        out_specs=out_specs,
        scratch_shapes=list(scratch),
        input_output_aliases=aliases,
        cost_estimate=pl.CostEstimate(flops=flops, bytes_accessed=flops // 8, transcendentals=0),
        compiler_params=pltpu.CompilerParams(vmem_limit_bytes=limit << 20),
    )


def per_device(state, base, dt, row_map, lag, count, jac, dis, freq):
    shape = state.shape
    x = state.reshape(45, 128, 128)
    b = base.reshape(45, 128, 128)
    dt = dt.reshape(128, 128)
    jac = jac.transpose(0, 2, 1, 3)
    x, b, dt, row_map, lag, count, dis, freq, jac = [
        pltpu.with_memory_space_constraint(a, pltpu.HBM)
        for a in (x, b, dt, row_map, lag, count, dis, freq, jac)
    ]
    quarter, rim = sds(2, 16, 128), sds(45, 8, 128)
    padded, whole = VMEM((45, 240, 128), F32), VMEM((45, 128, 128), F32)
    dma = pltpu.SemaphoreType.DMA
    pair = sds(2, 2, 16, 128)
    kept, sent, faces, x = call(
        faces_kernel, [pair, pair, sds(8, 16, 128), padded], [hspec()], [vspec()] * 4, [dma((8,))]
    )(x)
    other = swap(sent, 1)
    sent = call(pair_kernel, pair, [vspec()] * 2, vspec())(kept, other)
    far = swap(sent, 8)
    rims, rim_w, edge, forward, backward, mixing, coef, dt = call(
        leave_kernel,
        [sds(90, 8, 128), rim, sds(45, 16, 128), sds(96, 64)]
        + [sds(128, 64), sds(128, 128), sds(COEFS, 8, 128), sds(128, 128)],
        [hspec()] * 7 + [vspec()],
        [vspec()] * 8,
        [
            pltpu.SMEM((64,), jnp.int32),
            pltpu.SMEM((3,), jnp.int32),
            pltpu.SMEM((2,), jnp.int32),
            pltpu.SMEM((3, 3), F32),
            pltpu.SMEM((3,), F32),
            pltpu.SMEM((3, 5, 3, 5), F32),
            dma((7,)),
        ],
        flops=2000000,
    )(row_map, lag, count, dis, freq, jac, dt, x)
    from_span = lax.ppermute(edge, "span", [(0, 1), (1, 0)])
    modes = call(
        project_kernel, sds(2, 64, 128), [vspec()] * 4, vspec(), flops=1000000
    )(kept, other, far, forward)
    from_core = swap(rims, 1)
    from_chip = other_end(rims, [(i, i + 1) for i in range(1, 63, 2)])
    wraps = []
    for pairs in ENDS:
        wraps.append(other_end(rim_w, pairs))
    for n, mask in enumerate(HOPS):
        other = swap(modes, mask)
        if n < 3:
            modes = modes + other
    acc, b = call(
        functools.partial(along_first_kernel, *ALONG[0]),
        [whole, whole],
        [vspec()] * 2 + [hspec()],
        [vspec()] * 2,
        [dma],
        flops=10000000,
    )(coef, x, b)
    for first, last in ALONG[1:]:
        acc = call(
            functools.partial(along_kernel, first, last),
            whole,
            [vspec()] * 3,
            vspec(),
            flops=3000000 * (last - first),
            aliases={2: 0},
        )(coef, x, acc)
    x = call(
        ghosts_kernel, padded, [vspec()] * 7, vspec(), flops=1000000, aliases={6: 0}
    )(coef, from_core, from_chip, *wraps, from_span, x)
    for first, last in ACROSS:
        acc = call(
            functools.partial(across_kernel, first, last),
            whole,
            [vspec()] * 5,
            vspec(),
            flops=5000000 * (last - first),
            aliases={4: 0},
        )(coef, x, dt, b, acc)
    own, core, far = call(
        evaluate_kernel, [quarter, quarter, pair], [vspec()] * 3, [vspec()] * 3, flops=1000000
    )(modes, other, backward)
    far = swap(far, 8)
    core = call(pack_kernel, pair, [vspec()] * 2, vspec())(core, far)
    core = swap(core, 1)
    half = [VMEM((45, 64, 128), F32), VMEM((64, 128), F32), dma((5, 2))]
    acc, out = call(
        functools.partial(near_kernel, *LAST),
        [whole, sds(45, 128, 128)],
        [vspec()] * 9,
        [vspec(), hspec()],
        half,
        flops=15000000,
        aliases={4: 0},
    )(coef, x, dt, b, acc, own, far, faces, mixing)
    out = call(
        finish_kernel,
        sds(45, 128, 128),
        [vspec()] * 5 + [hspec()],
        hspec(),
        half,
        flops=5000000,
        aliases={5: 0},
    )(acc, core, faces, mixing, dt, out)
    return out.reshape(shape)


def solution(mesh):
    finer = Mesh(
        mesh.devices.reshape(4, 2, 4, 2, mesh.shape["span"]),
        ("blk_0", "blk_1", "blk_2", "blk_3", "span"),
    )
    return jax.shard_map(
        per_device,
        mesh=finer,
        in_specs=(
            P(None, None, "span", BLK, None),
            P(None, None, "span", BLK, None),
            P("span", BLK, None),
            P(),
            P(),
            P(),
            P(),
            P(),
            P(),
        ),
        out_specs=P(None, None, "span", BLK, None),
        check_vma=False,
    )
```

```python
import functools
import math

import jax
import jax.numpy as jnp
from jax import lax
from jax.experimental import pallas as pl
from jax.experimental.pallas import tpu as pltpu
from jax.sharding import Mesh
from jax.sharding import PartitionSpec as P

BLK = ("blk_0", "blk_1", "blk_2", "blk_3")
ENDS = (
    ((0, 32), (2, 34), (31, 63), (29, 61)),
    ((0, 28), (2, 30), (35, 63), (33, 61)),
)
EXACT = lax.Precision.HIGHEST
VMEM = pltpu.VMEM
F32 = jnp.float32
QUAD = (0, 1, 8, 9)
HOPS = (16, 48, 6, 2)
DN = tuple(0.5 * math.cos(math.pi * n) / math.sin(math.pi * n / 9) for n in range(5) if n)


ALONG = ((0, 5), (5, 8))
ACROSS = ((0, 4), (4, 8))
LAST = (8, 8)
CENTRE, WAVE, SPAN, LEFT, RIGHT, COEFS = 90, 91, 95, 97, 98, 99


def vspec():
    return pl.BlockSpec(memory_space=VMEM)


def hspec():
    return pl.BlockSpec(memory_space=pltpu.HBM)


def own_block():
    return (
        (lax.axis_index("blk_0") * 2 + lax.axis_index("blk_1")) * 4 + lax.axis_index("blk_2")
    ) * 2 + lax.axis_index("blk_3")


def lengths_of(order):
    n0 = jnp.where(order < 2, 2, jnp.where(order < 4, 33, 29))
    n1 = jnp.where(
        (order == 2) | (order == 4), 2, jnp.where((order == 0) | (order == 5), 33, 29)
    )
    return n0, n1


def place_in_row(order, block):
    n0, n1 = lengths_of(order)
    row = (block >= n0).astype(jnp.int32) + (block >= n0 + n1).astype(jnp.int32)
    begin = jnp.where(row == 0, 0, jnp.where(row == 1, n0, n0 + n1))
    total = jnp.where(row == 0, n0, jnp.where(row == 1, n1, 64 - n0 - n1))
    return row, block - begin, total


def sine_and_cosine(count, period):
    inverse = 1.0 / period
    rest = count - jnp.floor(count * inverse + 0.5) * period
    quarters = rest * (4.0 * inverse)
    turn = jnp.floor(quarters + 0.5)
    z = (quarters - turn) * (0.5 * math.pi)
    y = z * z
    sin = z * (1.0 + y * (-1 / 6 + y * (1 / 120 + y * (-1 / 5040 + y * (1 / 362880)))))
    cos = 1.0 + y * (
        -1 / 2 + y * (1 / 24 + y * (-1 / 720 + y * (1 / 40320 + y * (-1 / 3628800))))
    )
    turn = turn.astype(jnp.int32) & 3
    odd = (turn & 1) == 1
    sin, cos = jnp.where(odd, cos, sin), jnp.where(odd, sin, cos)
    return jnp.where(turn >= 2, -sin, sin), jnp.where((turn == 1) | (turn == 2), -cos, cos)


def order_of(rows):
    late = rows[31] == 2
    first = jnp.where(rows[2] == 1, 0, jnp.where(rows[29] == 0, 2, 4))
    second = jnp.where(
        first == 0,
        late.astype(jnp.int32),
        jnp.where(first == 2, (rows[35] != 2).astype(jnp.int32), 1 - late.astype(jnp.int32)),
    )
    return first + second


def waves(members):
    shape = (16, 128)
    lane = lax.broadcasted_iota(jnp.int32, shape, 1)
    mode = lax.broadcasted_iota(jnp.int32, shape, 0)
    member = (lane // 16) & 3

    def pick(n):
        values = [jnp.full(shape, m[n], jnp.int32) for m in members]
        return jnp.where(
            member < 2,
            jnp.where(member == 0, values[0], values[1]),
            jnp.where(member == 2, values[2], values[3]),
        )

    its_row = pick(0)
    period = (pick(2) * 32).astype(F32)
    odd = ((pick(1) * 16 + (lane & 15)) * 2 + 1).astype(F32)
    sin, cos = sine_and_cosine(mode.astype(F32) * odd, period)
    return its_row, lane, mode, period, cos, sin


def members_of(order):
    block = own_block()
    return [place_in_row(order, lax.bitwise_xor(block, m)) for m in QUAD]


def write_forward(its_waves, forward):
    its_row, _, mode, period, cos, sin = its_waves
    weight = jnp.where(mode == 0, 2.0, 4.0) / period
    for r in range(3):
        here = its_row == r
        forward[pl.ds(32 * r, 16), :] = jnp.where(here, cos * weight, 0.0)[:, :64]
        forward[pl.ds(32 * r + 16, 16), :] = jnp.where(here, sin * weight, 0.0)[:, :64]


def write_rest(block, members, its_waves, count, dis, freq, jac, backward, mixing, coef):
    row, position, total = members[0]
    far_end = jnp.where(total == 33, 2.0, 3.0)
    even = (block & 1) == 0
    to_next, to_last = jnp.where(even, 0.0, 1.0), jnp.where(even, 1.0, 0.0)
    before = jnp.where(position > 0, to_last, jnp.where(total == 2, to_next, far_end))
    after = jnp.where(position < total - 1, to_next, jnp.where(total == 2, to_last, far_end))
    its_row, lane, mode, _, cos, sin = its_waves
    seen = its_row - jnp.where(lane < 64, 1, 0)
    back = []
    for gap in range(2):
        kept = (seen == gap) & (mode < count[gap])
        back += [jnp.where(kept, cos, 0.0), jnp.where(kept, sin, 0.0)]
    backward[...] = jnp.concatenate(back, axis=0).T

    shape = (128, 128)
    source = lax.broadcasted_iota(jnp.int32, shape, 0)
    target = lax.broadcasted_iota(jnp.int32, shape, 1)

    def variable(ids):
        return sum((ids >= 18 * n).astype(jnp.int32) for n in range(1, 5))

    line = lax.broadcasted_iota(jnp.int32, (8, 128), 1)
    u_of = variable(line)
    v_of = variable(lax.broadcasted_iota(jnp.int32, (128, 1), 0))
    crossed = lax.bitwise_xor(target, 1)
    same = (crossed - 18 * u_of[:1]) == (source - 18 * v_of)
    terms = jnp.zeros(shape, F32)
    for v in range(5):
        entries = jnp.zeros((8, 128), F32)
        for u in range(5):
            entries = jnp.where(u_of == u, jac[row, u, 1, v], entries)
        terms = jnp.where(v_of == v, entries[:1], terms)
    terms = terms * jnp.where((source & 1) == 0, -0.5, 0.5)
    terms = terms - jnp.where(crossed == source, dis[row, 1], 0.0)
    mixing[...] = jnp.where(same & (source < 90), terms, 0.0)

    def put(at, value):
        coef[at] = jnp.full((8, 128), value, F32)

    for d in range(3):
        for u in range(5):
            for v in range(5):
                half = 0.5 * jac[row, u, d, v]
                if u == v:
                    put(75 + d * 5 + u, half - dis[row, d])
                    put(d * 25 + u * 5 + v, half + dis[row, d])
                else:
                    put(d * 25 + u * 5 + v, half)
    put(CENTRE, 2.0 * (dis[row, 0] + dis[row, 1] + dis[row, 2]))
    for n in range(4):
        put(WAVE + n, freq[row] * DN[n])
    upper = lax.axis_index("span")
    put(LEFT, before)
    put(RIGHT, after)
    put(SPAN, upper.astype(F32))
    put(SPAN + 1, (1 - upper).astype(F32))


def faces_kernel(x_hbm, kept, sent, faces, x, sem):
    copies = [
        pltpu.make_async_copy(
            x_hbm.at[:, pl.ds(16 * s, 16), :], x.at[:, pl.ds(24 * s + 32, 16), :], sem.at[s]
        )
        for s in range(8)
    ]
    for copy in copies:
        copy.start()
    lane = lax.broadcasted_iota(jnp.int32, (8, 128), 1) // 2
    for s in range(8):
        copies[s].wait()
        acc = [jnp.zeros((8, 128), F32) for _ in range(2)]
        for j in range(45):
            for h in range(2):
                turned = pltpu.roll(x[j, pl.ds(24 * s + 32 + 8 * h, 8), :], 2 * j + 1, 1)
                acc[h] = jnp.where(lane == j, turned, acc[h])
        for h in range(2):
            faces[s, pl.ds(8 * h, 8), :] = acc[h]
    core = lax.axis_index("blk_3")
    for y in range(2):
        kept[y] = faces[pl.ds(4 * y + 2 * core, 2)]
        sent[y] = faces[pl.ds(4 * y + 2 - 2 * core, 2)]


def pair_kernel(kept, other, sent):
    y = 1 - lax.axis_index("blk_1")
    sent[0] = kept[y]
    sent[1] = other[y]


def pack_kernel(first, second, sent):
    sent[0] = first[...]
    sent[1] = second[1]


def leave_kernel(
    rows_hbm, lag_hbm, count_hbm, dis_hbm, freq_hbm, jac_hbm, dt_hbm, x,
    rims, rim_w, edge, forward, backward, mixing, coef, dt,
    rows, lag, count, dis, freq, jac, sem,
):
    small = [
        pltpu.make_async_copy(a, b, sem.at[n])
        for n, (a, b) in enumerate(
            (
                (rows_hbm, rows), (lag_hbm, lag), (count_hbm, count),
                (dis_hbm, dis), (freq_hbm, freq), (jac_hbm, jac), (dt_hbm, dt),
            )
        )
    ]
    for copy in small:
        copy.start()
    outer = pl.multiple_of(jnp.where(lax.axis_index("span") == 0, 200, 32), 8)

    @pl.loop(0, 9)
    def _(k):
        for v in range(5):
            edge[v * 9 + k] = x[v * 9 + k, pl.ds(outer, 16), :]

    for copy in small:
        copy.wait()
    members = members_of(order_of(rows))
    its_waves = waves(members)
    write_forward(its_waves, forward)
    write_rest(own_block(), members, its_waves, count, dis, freq, jac, backward, mixing, coef)
    row, position, total = members[0]
    at_begin, at_final = position == 0, position == total - 1
    turn = jnp.where(at_begin, 9 - lag[row], lag[row])
    end = jnp.where(at_begin, 32, 47)
    turn_left = jnp.where(at_begin & (total == 2), turn, 0)
    turn_right = jnp.where(at_final & (total == 2), turn, 0)

    @pl.loop(0, 9)
    def _(k):
        for v in range(5):
            j = v * 9 + k
            rims[j] = x[v * 9 + lax.rem(k + turn_left, 9), pl.ds(32, 8, stride=24), :]
            rims[45 + j] = x[v * 9 + lax.rem(k + turn_right, 9), pl.ds(47, 8, stride=24), :]
            rim_w[j] = x[v * 9 + lax.rem(k + turn, 9), pl.ds(end, 8, stride=24), :]


def project_kernel(kept, other, far, forward, out):
    y = lax.axis_index("blk_1")
    even = lax.broadcasted_iota(jnp.int32, (32, 128), 1) % 2 == 0
    for i in range(2):
        columns = jnp.concatenate([kept[y, i], other[y, i], far[0, i], far[1, i]], axis=0)
        parts = jnp.dot(forward[...], columns, precision=EXACT, preferred_element_type=F32)
        low, mid, high = parts[:32], parts[32:64], parts[64:]
        out[i, pl.ds(0, 32), :] = jnp.where(even, low, mid)
        out[i, pl.ds(32, 32), :] = jnp.where(even, mid, high)


def evaluate_kernel(m0, m1, backward, own, core, far):
    even = lax.broadcasted_iota(jnp.int32, (64, 128), 1) % 2 == 0
    for i in range(2):
        modes = m0[i] + m1[i]
        both = jnp.dot(backward[...], modes, precision=EXACT, preferred_element_type=F32)
        ghost = jnp.where(even, both[:64], both[64:])
        own[i] = ghost[:16]
        core[i] = ghost[16:32]
        far[0, i] = ghost[32:48]
        far[1, i] = ghost[48:]


def cells_of(place):
    core = lax.axis_index("blk_3")
    return 2 * jnp.where(place < 4, core, 1 - core) + (place & 1) + 4 * ((place >> 1) & 1)


def ghosts_kernel(coef, core, chip, wrap0, wrap1, edge, x_in, x):
    left, right = coef[LEFT], coef[RIGHT]
    keep_low = jnp.concatenate([coef[SPAN]] * 2, axis=0)
    keep_high = jnp.concatenate([coef[SPAN + 1]] * 2, axis=0)

    @pl.loop(0, 9)
    def _(k):
        for v in range(5):
            j = v * 9 + k
            low, high = core[45 + j], core[j]
            low = jnp.where(left == 1, chip[45 + j], low)
            high = jnp.where(right == 1, chip[j], high)
            for w, wrap in ((2, wrap0), (3, wrap1)):
                low = jnp.where(left == w, wrap[j], low)
                high = jnp.where(right == w, wrap[j], high)
            x[j, pl.ds(31, 8, stride=24), :] = low
            x[j, pl.ds(48, 8, stride=24), :] = high
            x[j, pl.ds(8, 16), :] = edge[j] * keep_low
            x[j, pl.ds(224, 16), :] = edge[j] * keep_high


def across_kernel(first, last, coef, x, dt, base, out_in, out):
    @pl.loop(first, last)
    def _(place):
        s = cells_of(place)
        at = pl.multiple_of(24 * s + 32, 8)
        to = pl.multiple_of(16 * s, 16)
        for h in range(2):
            there = pl.ds(to + 8 * h, 8)
            step = dt[there, :]
            for k in range(9):
                acc, diffs = [], []
                for v in range(5):
                    j = v * 9 + k
                    pairs = [
                        (d, x[j, pl.ds(at + 8 * h + r, 8), :], x[j, pl.ds(at + 8 * h - r, 8), :])
                        for d, r in ((0, 1), (2, 24))
                    ]
                    diffs.append({d: plus - minus for d, plus, minus in pairs})
                    terms = [
                        plus * coef[75 + d * 5 + v] - minus * coef[d * 25 + v * 6]
                        for d, plus, minus in pairs
                    ]
                    acc.append(terms[0] + terms[1])
                for u in range(5):
                    j = u * 9 + k
                    total_u = out[j, there, :] + acc[u]
                    for d in (0, 2):
                        part = None
                        for v in range(5):
                            if v != u:
                                product = diffs[v][d] * coef[d * 25 + u * 5 + v]
                                part = product if part is None else part + product
                        total_u = total_u + part
                    out[j, there, :] = base[j, there, :] - step * total_u


def along_first_kernel(first, last, coef, x, base_hbm, out, base, sem):
    fetch = pltpu.make_async_copy(base_hbm, base, sem)
    fetch.start()
    along_kernel(first, last, coef, x, out)
    fetch.wait()


def along_kernel(first, last, coef, x, *refs):
    out = refs[-1]

    @pl.loop(first, last)
    def _(s):
        at = pl.multiple_of(24 * s + 32, 8)
        to = pl.multiple_of(16 * s, 16)
        for h in range(2):
            here, there = pl.ds(at + 8 * h, 8), pl.ds(to + 8 * h, 8)
            for u in range(5):
                line = [x[u * 9 + k, here, :] for k in range(9)]
                for k in range(9):
                    turn = [
                        (line[(k - n) % 9] - line[(k + n) % 9]) * coef[WAVE + n - 1]
                        for n in range(1, 5)
                    ]
                    turn.append(line[k] * coef[CENTRE])
                    out[u * 9 + k, there, :] = (turn[0] + turn[1]) + (turn[2] + turn[3]) + turn[4]
            for k in range(9):
                acc, diffs = [], []
                for v in range(5):
                    j = v * 9 + k
                    own = x[j, here, :]
                    plus, minus = pltpu.roll(own, 127, 1), pltpu.roll(own, 1, 1)
                    diffs.append(plus - minus)
                    acc.append(
                        out[j, there, :]
                        + (plus * coef[80 + v] - minus * coef[25 + v * 6])
                    )
                for u in range(5):
                    part = None
                    for v in range(5):
                        if v != u:
                            product = diffs[v] * coef[25 + u * 5 + v]
                            part = product if part is None else part + product
                    out[u * 9 + k, there, :] = acc[u] + part


def add_ghosts(places, refs, faces, mixing, dt, acc, stage, ghost, after):
    cells = [cells_of(p) for p in places]
    for n, (s, ref) in enumerate(zip(cells, refs)):
        ghost[pl.ds(16 * n, 16), :] = ref[...] - faces[s]
    terms = jnp.dot(ghost[...], mixing[...], precision=EXACT, preferred_element_type=F32)
    lane = lax.broadcasted_iota(jnp.int32, (16, 128), 1)
    rows = [pl.ds(pl.multiple_of(16 * s, 16), 16) for s in cells]
    steps = [jnp.where((lane == 0) | (lane == 127), dt[r, :], 0.0) for r in rows]
    for v in range(5):
        for j in range(9 * v, 9 * v + 9):
            turned = pltpu.roll(terms, 127 - 2 * j, 1)
            for n in range(4):
                stage[j, pl.ds(16 * n, 16), :] = (
                    acc[j, rows[n], :] - steps[n] * turned[16 * n : 16 * n + 16]
                )

        after(v)


def writes(stage, out_hbm, sem, first, variables):
    core = lax.axis_index("blk_3")
    core = core if first else 1 - core
    lines = pl.ds(9 * variables[0], 9 * len(variables))
    return [
        pltpu.make_async_copy(
            stage.at[lines, pl.ds(32 * n, 32), :],
            out_hbm.at[lines, pl.ds(pl.multiple_of(32 * core + 64 * n, 32), 32), :],
            sem.at[variables[0], n],
        )
        for n in range(2)
    ]


def near_kernel(
    first, last, coef, x, dt, base, acc_in, own, far, faces, mixing,
    acc, out_hbm, stage, ghost, sem,
):
    def send(v):
        for copy in writes(stage, out_hbm, sem, True, (v,)):
            copy.start()

    refs = []
    for half in range(2):
        mine = (lax.axis_index("blk_1") == half)
        for i in range(2):
            refs.append(jnp.where(mine, own[i], far[0, i]))
    add_ghosts(range(4), refs, faces, mixing, dt, acc, stage, ghost, send)
    across_kernel(first, last, coef, x, dt, base, None, acc)
    for v in range(5):
        for copy in writes(stage, out_hbm, sem, True, (v,)):
            copy.wait()


def finish_kernel(acc, core, faces, mixing, dt, out_in, out_hbm, stage, ghost, sem):
    def send(v):
        for copy in writes(stage, out_hbm, sem, False, (v,)):
            copy.start()

    refs = []
    for half in range(2):
        mine = (lax.axis_index("blk_1") == half)
        for i in range(2):
            refs.append(jnp.where(mine, core[0, i], core[1, i]))
    add_ghosts(range(4, 8), refs, faces, mixing, dt, acc, stage, ghost, send)
    for v in range(5):
        for copy in writes(stage, out_hbm, sem, False, (v,)):
            copy.wait()


def swap(x, mask):
    return lax.ppermute(x, BLK, [(i, i ^ mask) for i in range(64)])


def other_end(x, pairs):
    ends = dict(pairs) | {b: a for a, b in pairs}
    return lax.ppermute(x, BLK, [(i, ends.get(i, i)) for i in range(64)])


def sds(*shape, dtype=F32):
    return jax.ShapeDtypeStruct(shape, dtype)


def call(kernel, outs, in_specs, out_specs, scratch=(), limit=8, flops=0, aliases={}):
    return pl.pallas_call(
        kernel,
        out_shape=outs,
        in_specs=in_specs,
        out_specs=out_specs,
        scratch_shapes=list(scratch),
        input_output_aliases=aliases,
        cost_estimate=pl.CostEstimate(flops=flops, bytes_accessed=flops // 8, transcendentals=0),
        compiler_params=pltpu.CompilerParams(vmem_limit_bytes=limit << 20),
    )


def per_device(state, base, dt, row_map, lag, count, jac, dis, freq):
    shape = state.shape
    x = state.reshape(45, 128, 128)
    b = base.reshape(45, 128, 128)
    dt = dt.reshape(128, 128)
    jac = jac.transpose(0, 2, 1, 3)
    x, b, dt, row_map, lag, count, dis, freq, jac = [
        pltpu.with_memory_space_constraint(a, pltpu.HBM)
        for a in (x, b, dt, row_map, lag, count, dis, freq, jac)
    ]
    quarter, rim = sds(2, 16, 128), sds(45, 8, 128)
    padded, whole = VMEM((45, 240, 128), F32), VMEM((45, 128, 128), F32)
    dma = pltpu.SemaphoreType.DMA
    pair = sds(2, 2, 16, 128)
    kept, sent, faces, x = call(
        faces_kernel, [pair, pair, sds(8, 16, 128), padded], [hspec()], [vspec()] * 4, [dma((8,))]
    )(x)
    other = swap(sent, 1)
    sent = call(pair_kernel, pair, [vspec()] * 2, vspec())(kept, other)
    far = swap(sent, 8)
    rims, rim_w, edge, forward, backward, mixing, coef, dt = call(
        leave_kernel,
        [sds(90, 8, 128), rim, sds(45, 16, 128), sds(96, 64)]
        + [sds(128, 64), sds(128, 128), sds(COEFS, 8, 128), sds(128, 128)],
        [hspec()] * 7 + [vspec()],
        [vspec()] * 8,
        [
            pltpu.SMEM((64,), jnp.int32),
            pltpu.SMEM((3,), jnp.int32),
            pltpu.SMEM((2,), jnp.int32),
            pltpu.SMEM((3, 3), F32),
            pltpu.SMEM((3,), F32),
            pltpu.SMEM((3, 5, 3, 5), F32),
            dma((7,)),
        ],
        flops=2000000,
    )(row_map, lag, count, dis, freq, jac, dt, x)
    from_span = lax.ppermute(edge, "span", [(0, 1), (1, 0)])
    modes = call(
        project_kernel, sds(2, 64, 128), [vspec()] * 4, vspec(), flops=1000000
    )(kept, other, far, forward)
    from_core = swap(rims, 1)
    from_chip = other_end(rims, [(i, i + 1) for i in range(1, 63, 2)])
    wraps = []
    for pairs in ENDS:
        wraps.append(other_end(rim_w, pairs))
    for n, mask in enumerate(HOPS):
        other = swap(modes, mask)
        if n < 3:
            modes = modes + other
    acc, b = call(
        functools.partial(along_first_kernel, *ALONG[0]),
        [whole, whole],
        [vspec()] * 2 + [hspec()],
        [vspec()] * 2,
        [dma],
        flops=10000000,
    )(coef, x, b)
    for first, last in ALONG[1:]:
        acc = call(
            functools.partial(along_kernel, first, last),
            whole,
            [vspec()] * 3,
            vspec(),
            flops=3000000 * (last - first),
            aliases={2: 0},
        )(coef, x, acc)
    x = call(
        ghosts_kernel, padded, [vspec()] * 7, vspec(), flops=1000000, aliases={6: 0}
    )(coef, from_core, from_chip, *wraps, from_span, x)
    for first, last in ACROSS:
        acc = call(
            functools.partial(across_kernel, first, last),
            whole,
            [vspec()] * 5,
            vspec(),
            flops=5000000 * (last - first),
            aliases={4: 0},
        )(coef, x, dt, b, acc)
    own, core, far = call(
        evaluate_kernel, [quarter, quarter, pair], [vspec()] * 3, [vspec()] * 3, flops=1000000
    )(modes, other, backward)
    far = swap(far, 8)
    core = call(pack_kernel, pair, [vspec()] * 2, vspec())(core, far)
    core = swap(core, 1)
    half = [VMEM((45, 64, 128), F32), VMEM((64, 128), F32), dma((5, 2))]
    acc, out = call(
        functools.partial(near_kernel, *LAST),
        [whole, sds(45, 128, 128)],
        [vspec()] * 9,
        [vspec(), hspec()],
        half,
        flops=15000000,
        aliases={4: 0},
    )(coef, x, dt, b, acc, own, far, faces, mixing)
    out = call(
        finish_kernel,
        sds(45, 128, 128),
        [vspec()] * 5 + [hspec()],
        hspec(),
        half,
        flops=5000000,
        aliases={5: 0},
    )(acc, core, faces, mixing, dt, out)
    return out.reshape(shape)


def solution(mesh):
    finer = Mesh(
        mesh.devices.reshape(4, 2, 4, 2, mesh.shape["span"]),
        ("blk_0", "blk_1", "blk_2", "blk_3", "span"),
    )
    return jax.shard_map(
        per_device,
        mesh=finer,
        in_specs=(
            P(None, None, "span", BLK, None),
            P(None, None, "span", BLK, None),
            P("span", BLK, None),
            P(),
            P(),
            P(),
            P(),
            P(),
            P(),
        ),
        out_specs=P(None, None, "span", BLK, None),
        check_vma=False,
    )
```
